32 devices in a mesh: ctx: 8 (over z, x), tp: 4 (over y, core).
Axes of the slice: x: 2, y: 2, z: 4, core: 2. Of those that a mesh axis runs over, the one named last changes fastest.
Arguments:
- query_branch: bfloat16 [2048, 8192], P('ctx', 'tp'), may hold values from -6 to 6
- key_branch: bfloat16 [2048, 8192], P('ctx', 'tp'), may hold values from -6 to 6
- value_branch: bfloat16 [2048, 8192], P('ctx', 'tp'), may hold values from -6 to 6
- out_cotangent: bfloat16 [2048, 8192], P('ctx', 'tp'), may hold values from -6 to 6
- out_weight: bfloat16 [8192, 8192], P('tp', 'ctx'), may hold values from -0.09375 to 0.09375
- residues: float32 [512, 16], P('tp'), may hold values from -1.5 to 1.5
- decay_rates: float32 [512, 16], P('tp'), may hold values from 4.93164063e-05 to 0.0799
- skip_gains: float32 [8192], P('tp'), may hold values from 0.1 to 1.9
- record_lengths: int32 [24], replicated, may hold values from 1 to 512, 2048 in all
Outputs:
- block_output: bfloat16 [2048, 8192], P('ctx', 'tp')
- query_grad: bfloat16 [2048, 8192], P('ctx', 'tp')
- key_grad: bfloat16 [2048, 8192], P('ctx', 'tp')
- value_grad: bfloat16 [2048, 8192], P('ctx', 'tp')
The draws below stay inside these ranges and needn't reach their ends.
Inputs may be any that keep to these rules, and one draw needn't show every extreme that they name: record_lengths sum to 2048; the longest record has exactly 512 tokens.
All inputs are finite; a program needn't handle non-finite values.
Results may differ from the reference program's by a relative error of at most 0.006.
Values may be sent and summed in bfloat16 or wider, within the bound.
A program may use at most 128 MiB of HBM per device.

```python
import math
import jax
import jax.numpy as jnp
import numpy as np
from jax import lax

D = 8192
MODES = 16
GSIZE = 16
RECORDS = 24
SEQ = 2048
GROUPS = 512
RECORD_MAX = 512


def draw_decay_rates(key, part):
    grid_shape = (GROUPS, MODES)
    key_slow = jax.random.fold_in(key, 101)
    rate_values = jnp.exp(jax.random.uniform(key_slow, grid_shape, jnp.float32, math.log(0.3 / SEQ), math.log(0.0799)))
    return rate_values.astype(jnp.float32)


def strengthened(result, key, source, target, parts, factor):
    owner, partner = [(jnp.arange(result.shape[dim]) // (result.shape[dim] // parts)).reshape([-1 if axis == dim else 1 for axis in range(result.ndim)]) for dim in (source, target)]
    chosen = jax.random.permutation(key, parts)[partner]
    strong = (owner == chosen) | (owner == (partner + parts // 2) % parts)
    return jnp.where(strong, factor * result, result)


def block_levels(stream_key, dims, pieces, smallest, largest):
    factor_of = 1.0
    for dim, parts in pieces:
        steps = jax.random.uniform(jax.random.fold_in(jax.random.fold_in(stream_key, 6), dim), (parts,), jnp.float32, smallest / len(pieces), largest / len(pieces))
        factor_of = factor_of * jnp.repeat(jnp.exp(steps), dims[dim] // parts).reshape((-1,) + (1,) * (len(dims) - 1 - dim))
    return factor_of


def split_up(amount, total, most, skew):
    loads = [(1 << 20) // math.isqrt(standing ** skew) + 1 for standing in range(2, amount + 1)]
    spare, holding = total - most - (amount - 1), [1] * (amount - 1)
    while spare > 0:
        candidates = [i for i in range(amount - 1) if holding[i] < most]
        mass, left = sum([loads[i] for i in candidates]), spare
        for i in candidates:
            more = min(most - holding[i], max(1, left * loads[i] // mass), spare)
            holding[i] = holding[i] + more
            spare = spare - more
    return np.array([most] + holding)


def uneven_parts(stream_key, count, total, most, lean):
    if count == 2:
        one = jax.random.randint(stream_key, (), max(1, total - most), min(most, total - 1) + 1)
        return jnp.stack([one, total - one])
    lengths = jnp.asarray(split_up(count, total, most, lean), jnp.int32)
    twos = (count - 1) // 2
    source_of, receiver = lengths[1:1 + 2 * twos:2], lengths[2:2 + 2 * twos:2]
    margin = jnp.minimum(source_of - 1, most - receiver)
    shifted = jax.random.randint(jax.random.fold_in(stream_key, 1), (twos,), 0, 1 << 20) % (margin + 1)
    lengths = lengths.at[1:1 + 2 * twos:2].set(source_of - shifted).at[2:2 + 2 * twos:2].set(receiver + shifted)
    return lengths[jax.random.permutation(jax.random.fold_in(stream_key, 2), count)]


def bell_draw(rng, extent, spread, most, shards=(), held_as=jnp.bfloat16):
    array = jax.random.normal(rng, extent, jnp.float32) * spread
    if len(shards) > 0:
        array = block_levels(rng, extent, shards, -0.22, 0.18) * array
    return jnp.clip(array, min=-most, max=most).astype(held_as)


def gaussian_with(key, extent, width, reach, shards, heavy, held_as=jnp.bfloat16):
    drawn = width * jax.random.normal(key, extent, jnp.float32)
    if shards:
        drawn = drawn * block_levels(key, extent, shards, -0.22, 0.18)
    return jnp.clip(strengthened(drawn, jax.random.fold_in(key, 3), *heavy), -reach, reach).astype(held_as)


def setup_inputs(seed: int = 0) -> dict:
    streams_of = jax.random.split(jax.random.key(seed), 10)
    return {
        "query_branch": bell_draw(streams_of[0], (SEQ, D), 1.0, 6.0, ((0, 8), (1, 4))),
        "key_branch": bell_draw(streams_of[1], (SEQ, D), 1.0, 6.0, ((0, 8), (1, 4))),
        "value_branch": bell_draw(streams_of[2], (SEQ, D), 1.0, 6.0, ((0, 8), (1, 4))),
        "out_cotangent": bell_draw(streams_of[3], (SEQ, D), 1.0, 6.0, ((0, 8), (1, 4))),
        "out_weight": gaussian_with(streams_of[4], (D, D), D ** -0.5, 0.09375, ((0, 4), (1, 8)), (0, 1, 8, 2.0)),
        "residues": bell_draw(streams_of[5], (GROUPS, MODES), MODES ** -0.5, 1.5, ((0, 4),), jnp.float32),
        "decay_rates": draw_decay_rates(jax.random.fold_in(streams_of[9], 71), 0),
        "skip_gains": jnp.clip(1.0 + 0.18 * jax.random.normal(streams_of[7], (D,), jnp.float32), 0.1, 1.9),
        "record_lengths": uneven_parts(streams_of[8], RECORDS, SEQ, RECORD_MAX, 2).astype(jnp.int32),
    }


def reference(query_branch, key_branch, value_branch, out_cotangent, out_weight, residues, decay_rates, skip_gains, record_lengths):
    seq_len = query_branch.shape[0]
    offsets = jnp.cumsum(record_lengths) - record_lengths
    position = jnp.arange(seq_len, dtype=jnp.int32)
    is_start = jnp.any(position[:, None] == offsets[None, :], axis=1)
    keep = jnp.where(is_start, 0.0, 1.0).astype(jnp.float32)
    gated = (key_branch.astype(jnp.float32) * value_branch.astype(jnp.float32)).astype(jnp.bfloat16)
    decay_chan = jnp.repeat(jnp.exp(-decay_rates).T, GSIZE, axis=1)
    coeffs = residues * jnp.sqrt(1.0 - jnp.exp(-2.0 * decay_rates))
    coeff_chan = jnp.repeat(coeffs.T, GSIZE, axis=1)

    def forward_step(carried, inputs):
        gated_row, keep_row = inputs
        carried = decay_chan * keep_row * carried + gated_row[None, :]
        return (carried, lax.optimization_barrier(jnp.sum(coeff_chan * carried, axis=0)))
    unused, filt_sum = lax.scan(forward_step, jnp.zeros((MODES, D), jnp.float32), (gated.astype(jnp.float32), keep))
    filtered = lax.optimization_barrier(filt_sum.astype(jnp.bfloat16)).astype(jnp.float32)
    mixed = filtered + skip_gains[None, :] * gated.astype(jnp.float32)
    mixer_out = (query_branch.astype(jnp.float32) * mixed).astype(jnp.bfloat16)
    block_output = jnp.dot(mixer_out, out_weight, preferred_element_type=jnp.float32).astype(jnp.bfloat16)
    mixer_grad = jnp.dot(out_cotangent, out_weight.T, preferred_element_type=jnp.float32).astype(jnp.bfloat16)
    mixer_grad = lax.optimization_barrier(mixer_grad).astype(jnp.float32)
    filter_grad = (mixer_grad * query_branch.astype(jnp.float32)).astype(jnp.bfloat16)
    query_grad = (mixer_grad * mixed).astype(jnp.bfloat16)

    def adjoint_step(message, inputs):
        grad_row, keep_row = inputs
        adjoint = coeff_chan * grad_row[None, :] + message
        return (decay_chan * keep_row * adjoint, lax.optimization_barrier(jnp.sum(adjoint, axis=0)))
    unused_msg, adj_total = lax.scan(adjoint_step, jnp.zeros((MODES, D), jnp.float32), (filter_grad.astype(jnp.float32), keep), reverse=True)
    adjoint_sum = lax.optimization_barrier(adj_total.astype(jnp.bfloat16)).astype(jnp.float32)
    gated_grad = adjoint_sum + skip_gains[None, :] * filter_grad.astype(jnp.float32)
    key_grad = (gated_grad * value_branch.astype(jnp.float32)).astype(jnp.bfloat16)
    value_grad = (gated_grad * key_branch.astype(jnp.float32)).astype(jnp.bfloat16)
    return (block_output, query_grad, key_grad, value_grad)
```

```python
import functools

import jax
import jax.numpy as jnp
from jax import lax
from jax.experimental import pallas as pl
from jax.experimental.pallas import tpu as pltpu
from jax.sharding import Mesh, PartitionSpec as P

GSIZE = 16
LANES = 128
TILE_GROUPS = LANES // GSIZE
CORES = 2
COLS = 256
F32, BF16 = jnp.float32, jnp.bfloat16
MESH = pl.DeviceIdType.MESH


def split(a):
    hi = a.astype(BF16)
    return hi, (a - hi.astype(F32)).astype(BF16)


def wide(block, length):
    return jnp.concatenate([block[...]] * (length // LANES), axis=1)


def positions(rows, length):
    return lax.broadcasted_iota(jnp.int32, (rows, length), 1).astype(F32)


def inflow_rows(rates, coeffs, pos, first):
    return coeffs * jnp.exp(-rates * (pos + 1.0)) * first


def outflow_rows(rates, pos, last):
    return jnp.exp(-rates * (pos.shape[1] - 1.0 - pos)) * last


def own_lanes(shape, group):
    lane = lax.broadcasted_iota(jnp.int32, shape, 1)
    return (lane >= group * GSIZE) & (lane < (group + 1) * GSIZE)


def weighted_state(rows, x, modes):
    hi, lo = split(rows)
    full = jnp.dot(hi, x, preferred_element_type=F32) + jnp.dot(lo, x, preferred_element_type=F32)
    state = jnp.zeros((modes, LANES), F32)
    for g in range(TILE_GROUPS):
        part = full[g * modes : (g + 1) * modes]
        state = jnp.where(own_lanes(part.shape, g), part, state)
    return state


def contract_first(a, b):
    return lax.dot_general(a, b, (((0,), (0,)), ((), ())), preferred_element_type=F32)


def from_state(rows, state, modes):
    blocks = [
        jnp.where(own_lanes(state.shape, g), state, 0.0) for g in range(TILE_GROUPS)
    ]
    state_rows = jnp.concatenate(blocks, axis=0)
    r_hi, r_lo = split(rows)
    s_hi, s_lo = split(state_rows)
    return contract_first(r_hi, s_hi) + contract_first(r_lo, s_hi) + contract_first(r_hi, s_lo)


def convolve(left, right, mask, x, modes):
    l_hi, l_lo = split(left)
    r_hi, r_lo = split(right)
    total = jnp.zeros(x.shape, F32)
    for g in range(TILE_GROUPS):
        rows = slice(g * modes, (g + 1) * modes)
        a = jnp.concatenate([l_hi[rows], l_lo[rows], l_hi[rows]], axis=0)
        b = jnp.concatenate([r_hi[rows], r_hi[rows], r_lo[rows]], axis=0)
        kernel = (contract_first(a, b) * mask).astype(BF16)
        part = jnp.dot(kernel, x, preferred_element_type=F32)
        total = jnp.where(own_lanes(x.shape, g), part, total)
    return total


def gated_of(key, value):
    return (key[...].astype(F32) * value[...].astype(F32)).astype(BF16)


def forward_state(modes, key, value, rates, last, out):
    length = key.shape[0]
    pos = positions(rates.shape[0], length)
    rows = outflow_rows(wide(rates, length), pos, last[...])
    out[...] = weighted_state(rows, gated_of(key, value), modes)


def forward_filter(modes, key, value, query, skip, rates, coeffs, first, mask, state, mixed, mixer):
    length = key.shape[0]
    pos = positions(rates.shape[0], length)
    r, c = wide(rates, length), wide(coeffs, length)
    x = gated_of(key, value)
    half = length / 2.0
    left = c * jnp.exp(-r * (pos - half))
    right = jnp.exp(r * (pos - half))
    total = convolve(left, right, mask[...], x, modes)
    total = total + from_state(inflow_rows(r, c, pos, first[...]), state[...], modes)
    result = total.astype(BF16).astype(F32) + skip[...] * x.astype(F32)
    mixed[...] = result
    mixer[...] = (query[...].astype(F32) * result).astype(BF16)


def adjoint_state(modes, grad, query, mixed, rates, coeffs, first, filter_grad, query_grad, out):
    length = grad.shape[0]
    pos = positions(rates.shape[0], length)
    r, c = wide(rates, length), wide(coeffs, length)
    g = grad[...].astype(F32)
    f = (g * query[...].astype(F32)).astype(BF16)
    filter_grad[...] = f
    query_grad[...] = (g * mixed[...]).astype(BF16)
    out[...] = weighted_state(inflow_rows(r, c, pos, first[...]), f, modes)


def adjoint_filter(modes, grad, key, value, skip, rates, coeffs, last, mask, state, key_grad, value_grad):
    length = grad.shape[0]
    pos = positions(rates.shape[0], length)
    r, c = wide(rates, length), wide(coeffs, length)
    f = grad[...]
    half = length / 2.0
    left = jnp.exp(r * (pos - half))
    right = c * jnp.exp(-r * (pos - half))
    total = convolve(left, right, mask[...], f, modes)
    total = total + from_state(outflow_rows(r, pos, last[...]), state[...], modes)
    result = total.astype(BF16).astype(F32) + skip[...] * f.astype(F32)
    key_grad[...] = (result * value[...].astype(F32)).astype(BF16)
    value_grad[...] = (result * key[...].astype(F32)).astype(BF16)


def tiled_call(body, modes, kinds, operands, outs, length, channels, flops):
    rows = TILE_GROUPS * modes
    specs = {
        "tok": pl.BlockSpec((length, LANES), lambda i: (0, i)),
        "par": pl.BlockSpec((rows, LANES), lambda i: (i, 0)),
        "row": pl.BlockSpec((1, length), lambda i: (0, 0)),
        "skip": pl.BlockSpec((1, LANES), lambda i: (0, i)),
        "mask": pl.BlockSpec((length, length), lambda i: (0, 0)),
        "state": pl.BlockSpec((modes, LANES), lambda i: (0, i)),
    }
    shapes = {"tok": (length, channels), "state": (modes, channels)}
    moved = sum(o.size * o.dtype.itemsize for o in operands)
    return pl.pallas_call(
        functools.partial(body, modes),
        grid=(channels // LANES,),
        in_specs=[specs[k] for k in kinds],
        out_specs=[specs[k] for k, _ in outs],
        out_shape=[jax.ShapeDtypeStruct(shapes[k], d) for k, d in outs],
        cost_estimate=pl.CostEstimate(flops=flops, bytes_accessed=moved, transcendentals=0),
    )(*operands)


def when(cond):
    return pl.when(cond)


def exchange(sizes, mix, cot, w, yout, grad, wg, dyg, part, sbuf, rbuf, xg, yas, yar, ybs, ybr, yp, yf, yfs, yfr,
             wss, wrs, css, crs, gss, grs, fss, frs, xss, xrs, dss, drs, ass, ars, bss, brs, yss, yrs):
    nz, nx, ny = sizes
    length, channels = mix.shape
    width = w.shape[1]
    nk = channels // COLS
    nw = width // COLS
    halves = 2
    hrows = length // halves
    z, x = lax.axis_index("z"), lax.axis_index("x")
    y, c = lax.axis_index("y"), lax.axis_index("c")
    t = y * CORES + c
    across = (t, x, lax.div(z, CORES), lax.rem(z, CORES))
    twin = (z, x, y, 1 - c)

    def cp(src, dst, ssem, rsem, dev):
        return pltpu.make_async_remote_copy(
            src_ref=src, dst_ref=dst, send_sem=ssem, recv_sem=rsem, device_id=dev, device_id_type=MESH
        )

    def cols(i):
        return pl.ds(pl.multiple_of(i * COLS, COLS), COLS)

    barrier = pltpu.get_barrier_semaphore()
    for dx in range(1, nx):
        pl.semaphore_signal(barrier, 1, device_id=(z, lax.rem(x + dx, nx), y, c), device_id_type=MESH)
    for dy in range(1, ny):
        pl.semaphore_signal(barrier, 1, device_id=(z, x, lax.rem(y + dy, ny), c), device_id_type=MESH)
    pl.semaphore_signal(barrier, 1, device_id=twin, device_id_type=MESH)

    @when(z > 0)
    def _():
        pl.semaphore_signal(barrier, 1, device_id=(z - 1, x, y, c), device_id_type=MESH)

    @when(z < nz - 1)
    def _():
        pl.semaphore_signal(barrier, 1, device_id=(z + 1, x, y, c), device_id_type=MESH)

    @when(t != z)
    def _():
        pl.semaphore_signal(barrier, 1, device_id=across, device_id_type=MESH)

    pl.semaphore_wait(
        barrier,
        (nx - 1) + (ny - 1) + 1 + (z > 0).astype(jnp.int32) + (z < nz - 1).astype(jnp.int32) + (t != z).astype(jnp.int32),
    )

    def w_copy(d, k):
        rows = cols(k)
        return cp(w.at[rows], wg.at[d - 1, rows], wss.at[d - 1, k], wrs.at[d - 1, k], (z, lax.rem(x + d, nx), y, c))

    def half(h):
        return pl.ds(h * hrows, hrows)

    def cot_copy(h):
        return cp(cot.at[half(h)], dyg.at[z, half(h)], css.at[h], crs.at[h], across)

    def cot_arrival(h):
        return cp(cot.at[half(h)], dyg.at[t, half(h)], css.at[h], crs.at[h], across)

    def spread(d, h):
        dev = twin if d == 0 else (z, x, lax.rem(y + d, ny), c)
        return cp(dyg.at[t, half(h)], dyg.at[t, half(h)], gss.at[d, h], grs.at[d, h], dev)

    def spread_arrival(d, h):
        slot = y * CORES + 1 - c if d == 0 else lax.rem(y + ny - d, ny) * CORES + c
        return slot, cp(dyg.at[slot, half(h)], dyg.at[slot, half(h)], gss.at[d, h], grs.at[d, h], twin)

    def relay(d, h):
        slot = lax.rem(y + ny - d, ny) * CORES + c
        return cp(dyg.at[slot, half(h)], dyg.at[slot, half(h)], fss.at[d - 1, h], frs.at[d - 1, h], twin)

    def relay_arrival(d, h):
        slot = lax.rem(y + ny - d, ny) * CORES + 1 - c
        return cp(dyg.at[slot, half(h)], dyg.at[slot, half(h)], fss.at[d - 1, h], frs.at[d - 1, h], twin)

    def x_copy(up, o, j):
        dev = (z + 1, x, y, c) if up else (z - 1, x, y, c)
        side = 0 if up else 1
        return cp(xg.at[o, :, cols(j)], xg.at[o, :, cols(j)], xss.at[side, o, j], xrs.at[o, j], dev)

    def d_copy(up, o, k):
        dev = (z + 1, x, y, c) if up else (z - 1, x, y, c)
        slot = o + 1 if up else o
        return cp(sbuf.at[o, k], rbuf.at[slot, k], dss.at[o, k], drs.at[slot, k], dev)

    def a_copy(o, q):
        slot = lax.div(o, CORES)
        return cp(yas.at[slot, :, cols(q)], yar.at[slot, :, cols(q)], ass.at[slot, q], ars.at[slot, q], twin)

    def b_copy(yd, q):
        slot = lax.rem(yd + ny - y, ny) - 1
        return cp(ybs.at[slot, :, cols(q)], ybr.at[slot, :, cols(q)], bss.at[slot, q], brs.at[slot, q], (z, x, yd, c))

    def y_copy(q):
        return cp(yfs.at[:, cols(q)], yfr.at[:, cols(q)], yss.at[q], yrs.at[q], across)

    @when(t != z)
    def _():
        for h in range(halves):
            cot_copy(h).start()

    @when(t == z)
    def _():
        dyg[z] = cot[...]

    def start_w(k, _):
        for d in range(1, nx):
            w_copy(d, k).start()
        return 0

    lax.fori_loop(0, nk, start_w, 0)

    def start_x(j, _):
        xg[z, :, cols(j)] = mix[:, cols(j)]

        @when(z < nz - 1)
        def _():
            x_copy(True, z, j).start()

        @when(z > 0)
        def _():
            x_copy(False, z, j).start()

        return 0

    lax.fori_loop(0, nk, start_x, 0)

    for h in range(halves):
        @when(t != z)
        def _():
            cot_arrival(h).wait_recv()

        for d in range(ny):
            spread(d, h).start()

    for h in range(halves):
        for d in range(1, ny):
            spread_arrival(d, h)[1].wait_recv()
            relay(d, h).start()
        spread_arrival(0, h)[1].wait_recv()
        for d in range(1, ny):
            relay_arrival(d, h).wait_recv()

    def valid(k):
        return (k >= 0) & (k < nk)

    lag = jnp.maximum(z, nz - 1 - z)

    def step(s, _):
        for h in range(1, nz):
            j = s - (h - 1)
            for up in (True, False):
                o = z - h if up else z + h
                there = (o >= 0) if up else (o < nz)
                further = (z < nz - 1) if up else (z > 0)

                @when(valid(j) & there)
                def _():
                    x_copy(up, o, j).wait_recv()

                    @when(further)
                    def _():
                        x_copy(up, o, j).start()

        @when(s < nk)
        def _():
            for d in range(1, nx):
                w_copy(d, s).wait_recv()
            own_cols = pl.ds(pl.multiple_of(x * width, LANES), width)

            def rows_of(o, _):
                total = lax.dot_general(
                    dyg[o, :, own_cols], w[cols(s), :], (((1,), (1,)), ((), ())), preferred_element_type=F32
                )
                for d in range(1, nx):
                    from_cols = pl.ds(pl.multiple_of(lax.rem(x + nx - d, nx) * width, LANES), width)
                    total = total + lax.dot_general(
                        dyg[o, :, from_cols], wg[d - 1, cols(s), :], (((1,), (1,)), ((), ())), preferred_element_type=F32
                    )
                part[s, o] = total
                return 0

            lax.fori_loop(0, nz, rows_of, 0)

        up_k = s - z

        @when(valid(up_k) & (z < nz - 1))
        def _():
            for o in range(nz - 1, 0, -1):
                @when(o > z)
                def _():
                    @when(z > 0)
                    def _():
                        d_copy(True, o, up_k).wait_recv()
                        sbuf[o, up_k] = (part[up_k, o] + rbuf[o + 1, up_k].astype(F32)).astype(BF16)

                    @when(z == 0)
                    def _():
                        sbuf[o, up_k] = part[up_k, o].astype(BF16)

                    d_copy(True, o, up_k).start()

        down_k = s - (nz - 1 - z)

        @when(valid(down_k) & (z > 0))
        def _():
            for o in range(nz - 1):
                @when(o < z)
                def _():
                    @when(z < nz - 1)
                    def _():
                        d_copy(False, o, down_k).wait_recv()
                        sbuf[o, down_k] = (part[down_k, o] + rbuf[o, down_k].astype(F32)).astype(BF16)

                    @when(z == nz - 1)
                    def _():
                        sbuf[o, down_k] = part[down_k, o].astype(BF16)

                    d_copy(False, o, down_k).start()

        own_k = s - lag

        @when(valid(own_k))
        def _():
            yp[:, :COLS] = part[own_k, z]

            @when(z > 0)
            def _():
                d_copy(True, z, own_k).wait_recv()
                yp[:, :COLS] += rbuf[z + 1, own_k].astype(F32)

            @when(z < nz - 1)
            def _():
                d_copy(False, z, own_k).wait_recv()
                yp[:, :COLS] += rbuf[z, own_k].astype(F32)

            grad[:, cols(own_k)] = yp[:, :COLS].astype(BF16)

        return 0

    lax.fori_loop(0, nk + nz - 1, step, 0)

    def block(o):
        slot = lax.div(o, CORES)
        core, yd = lax.rem(o, CORES), lax.div(o, CORES)

        for src in range(nx):
            def column(i, _):
                q = lax.rem(x + nx - src, nx) * nw + i
                ref = w if src == 0 else wg.at[src - 1]
                p = jnp.dot(xg[o], ref[:, cols(i)], preferred_element_type=F32)

                @when(c != core)
                def _():
                    yas[slot, :, cols(q)] = p.astype(BF16)
                    a_copy(o, q).start()

                @when(c == core)
                def _():
                    yp[:, cols(q)] = p

                return 0

            lax.fori_loop(0, nw, column, 0)

        @when(c == core)
        def _():
            def add(i, _):
                q = lax.rem(x * nw + i, nk)
                a_copy(o, q).wait_recv()
                total = yp[:, cols(q)] + yar[slot, :, cols(q)].astype(F32)

                @when(yd != y)
                def _():
                    ybs[lax.rem(yd + ny - y, ny) - 1, :, cols(q)] = total.astype(BF16)
                    b_copy(yd, q).start()

                @when(yd == y)
                def _():
                    yf[:, cols(q)] = total

                return 0

            lax.fori_loop(0, nk, add, 0)

    def finish():
        def one(i, _):
            q = lax.rem(x * nw + i, nk)
            total = yf[:, cols(q)]
            for d in range(1, ny):
                cp(ybs.at[d - 1, :, cols(q)], ybr.at[d - 1, :, cols(q)], bss.at[d - 1, q], brs.at[d - 1, q], twin).wait_recv()
                total = total + ybr[d - 1, :, cols(q)].astype(F32)

            yfs[:, cols(q)] = total.astype(BF16)

            @when(t != z)
            def _():
                y_copy(q).start()

            return 0

        lax.fori_loop(0, nk, one, 0)

    block(z)
    for h in range(1, nz):
        @when(z + h < nz)
        def _():
            block(z + h)

        @when(z - h >= 0)
        def _():
            block(z - h)

        @when((t - z == h - 1) | (z - t == h - 1))
        def _():
            finish()

    @when((t - z == nz - 1) | (z - t == nz - 1))
    def _():
        finish()

    @when(t == z)
    def _():
        yout[...] = yfs[...]

    @when(t != z)
    def _():
        def land(q, _):
            y_copy(q).wait()
            return 0

        lax.fori_loop(0, nk, land, 0)
        yout[...] = yfr[...]
        for h in range(halves):
            cot_copy(h).wait_send()

    for h in range(halves):
        for d in range(ny):
            spread(d, h).wait_send()
        for d in range(1, ny):
            relay(d, h).wait_send()

    def drain(k, _):
        for d in range(1, nx):
            w_copy(d, k).wait_send()
        for slot in range(ny):
            a_copy(slot * CORES + 1 - c, k).wait_send()
        for d in range(1, ny):
            b_copy(lax.rem(y + d, ny), k).wait_send()
        for o in range(nz):
            @when((z < nz - 1) & (o <= z))
            def _():
                x_copy(True, o, k).wait_send()

            @when((z > 0) & (o >= z))
            def _():
                x_copy(False, o, k).wait_send()

            @when(o > z)
            def _():
                d_copy(True, o, k).wait_send()

            @when(o < z)
            def _():
                d_copy(False, o, k).wait_send()

        return 0

    lax.fori_loop(0, nk, drain, 0)


def exchanged(sizes, mixer, cot, weight):
    nz, nx, ny = sizes
    length, channels = mixer.shape
    width = weight.shape[1]
    nk = channels // COLS
    vmem = pl.BlockSpec(memory_space=pltpu.VMEM)
    token = jax.ShapeDtypeStruct((length, channels), BF16)
    dma = pltpu.SemaphoreType.DMA
    near = max(ny - 1, 1)
    wide_x = max(nx - 1, 1)
    flops = 8 * nz * length * channels * width * nx // 2
    return pl.pallas_call(
        functools.partial(exchange, sizes),
        out_shape=(token, token),
        in_specs=[vmem] * 3,
        out_specs=(vmem, vmem),
        scratch_shapes=[
            pltpu.VMEM((wide_x, channels, width), BF16),
            pltpu.VMEM((nz, length, channels), BF16),
            pltpu.VMEM((nk, nz, length, COLS), F32),
            pltpu.VMEM((nz, nk, length, COLS), BF16),
            pltpu.VMEM((nz + 1, nk, length, COLS), BF16),
            pltpu.VMEM((nz, length, channels), BF16),
            pltpu.VMEM((ny, length, channels), BF16),
            pltpu.VMEM((ny, length, channels), BF16),
            pltpu.VMEM((near, length, channels), BF16),
            pltpu.VMEM((near, length, channels), BF16),
            pltpu.VMEM((length, channels), F32),
            pltpu.VMEM((length, channels), F32),
            pltpu.VMEM((length, channels), BF16),
            pltpu.VMEM((length, channels), BF16),
            dma((wide_x, nk)), dma((wide_x, nk)),
            dma((2,)), dma((2,)),
            dma((ny, 2)), dma((ny, 2)),
            dma((near, 2)), dma((near, 2)),
            dma((2, nz, nk)), dma((nz, nk)),
            dma((nz, nk)), dma((nz + 1, nk)),
            dma((ny, nk)), dma((ny, nk)),
            dma((near, nk)), dma((near, nk)),
            dma((nk,)), dma((nk,)),
        ],
        compiler_params=pltpu.CompilerParams(
            collective_id=0, has_side_effects=True, vmem_limit_bytes=62 * 2**20
        ),
        cost_estimate=pl.CostEstimate(flops=flops, bytes_accessed=16 * 2**20, transcendentals=0),
    )(mixer, cot, weight)


def on_device(
    query_branch,
    key_branch,
    value_branch,
    out_cotangent,
    out_weight,
    residues,
    decay_rates,
    skip_gains,
    record_lengths,
):
    length, channels = query_branch.shape
    modes = residues.shape[1]
    nz, nx, ny = lax.axis_size("z"), lax.axis_size("x"), lax.axis_size("y")
    ctx = nz * nx
    hops = -(-(length * ctx // 4) // length)
    index = lax.axis_index("z") * nx + lax.axis_index("x")

    records = record_lengths.shape[0]
    before = jnp.arange(records)[:, None] > jnp.arange(records)[None, :]
    offsets = jnp.sum(jnp.where(before, record_lengths[None, :], 0), axis=1)
    blocks = jnp.arange(ctx, dtype=jnp.int32) * length
    closed = jnp.any(
        (offsets[None, :] >= blocks[:, None]) & (offsets[None, :] < blocks[:, None] + length), axis=1
    ).astype(jnp.int32)
    at = jnp.arange(length, dtype=jnp.int32)
    local = offsets - index * length

    def segment_of(pos):
        shape = (1,) * pos.ndim
        starts = local.reshape((-1,) + shape)
        return jnp.sum(((starts >= 0) & (starts <= pos[None])).astype(jnp.int32), axis=0)

    segment = segment_of(at)
    final = jnp.sum(((local >= 0) & (local < length)).astype(jnp.int32))
    first = (segment == 0).astype(F32)[None, :]
    last = (segment == final).astype(F32)[None, :]
    mask = ((at[:, None] >= at[None, :]) & (segment[:, None] == segment[None, :])).astype(F32)

    coeffs = residues * jnp.sqrt(1.0 - jnp.exp(-2.0 * decay_rates))
    rates_rows = jnp.broadcast_to(decay_rates.reshape(-1, 1), (decay_rates.size, LANES))
    coeff_rows = jnp.broadcast_to(coeffs.reshape(-1, 1), (coeffs.size, LANES))
    through = jnp.repeat(jnp.exp(-decay_rates * length).T, GSIZE, axis=1)
    skip = skip_gains[None, :]
    tiles = channels // LANES
    conv_flops = tiles * TILE_GROUPS * 2 * length * length * 512
    state_flops = tiles * 2 * 256 * 256 * length

    def gathered_state(state, direction):
        total = jnp.zeros_like(state)
        factor = jnp.ones_like(state)
        for hop in range(1, hops + 1):
            pairs = [
                (c, c + direction * hop) for c in range(ctx) if 0 <= c + direction * hop < ctx
            ]
            total = total + factor * lax.ppermute(state, ("z", "x"), pairs)
            passed = jnp.clip(index - direction * hop, 0, ctx - 1)
            open_here = 1.0 - closed[passed].astype(F32)
            factor = factor * through * open_here
        return total

    (own,) = tiled_call(
        forward_state, modes, ("tok", "tok", "par", "row"),
        (key_branch, value_branch, rates_rows, last),
        (("state", F32),), length, channels, state_flops,
    )
    entering = gathered_state(own, 1)
    mixed, mixer_out = tiled_call(
        forward_filter, modes,
        ("tok", "tok", "tok", "skip", "par", "par", "row", "mask", "state"),
        (key_branch, value_branch, query_branch, skip, rates_rows, coeff_rows, first, mask, entering),
        (("tok", F32), ("tok", BF16)), length, channels, conv_flops,
    )
    block_output, mixer_grad = exchanged((nz, nx, ny), mixer_out, out_cotangent, out_weight)

    filter_grad, query_grad, own = tiled_call(
        adjoint_state, modes, ("tok", "tok", "tok", "par", "par", "row"),
        (mixer_grad, query_branch, mixed, rates_rows, coeff_rows, first),
        (("tok", BF16), ("tok", BF16), ("state", F32)), length, channels, state_flops,
    )
    entering = gathered_state(own, -1)
    key_grad, value_grad = tiled_call(
        adjoint_filter, modes,
        ("tok", "tok", "tok", "skip", "par", "par", "row", "mask", "state"),
        (filter_grad, key_branch, value_branch, skip, rates_rows, coeff_rows, last, mask.T, entering),
        (("tok", BF16), ("tok", BF16)), length, channels, conv_flops,
    )
    return (block_output, query_grad, key_grad, value_grad)


def solution(mesh):
    ctx, tp = mesh.devices.shape
    fine = Mesh(mesh.devices.reshape(tp, ctx // tp, tp // CORES, CORES), ("z", "x", "y", "c"))
    tokens = P(("z", "x"), ("y", "c"))
    placed = (
        tokens,
        tokens,
        tokens,
        tokens,
        P(("y", "c"), ("z", "x")),
        P(("y", "c"), None),
        P(("y", "c"), None),
        P(("y", "c")),
        P(),
    )
    return jax.shard_map(
        on_device,
        mesh=fine,
        in_specs=placed,
        out_specs=(tokens, tokens, tokens, tokens),
        check_vma=False,
    )
```

```python
import functools

import jax
import jax.numpy as jnp
from jax import lax
from jax.experimental import pallas as pl
from jax.experimental.pallas import tpu as pltpu
from jax.sharding import Mesh, PartitionSpec as P

GSIZE = 16
LANES = 128
TILE_GROUPS = LANES // GSIZE
CORES = 2
COLS = 256
F32, BF16 = jnp.float32, jnp.bfloat16
MESH = pl.DeviceIdType.MESH


def split(a):
    hi = a.astype(BF16)
    return hi, (a - hi.astype(F32)).astype(BF16)


def positions(rows, length):
    return lax.broadcasted_iota(jnp.int32, (rows, length), 1).astype(F32)


def inflow_rows(rates, coeffs, pos, first):
    return coeffs * jnp.exp(-rates * (pos + 1.0)) * first


def outflow_rows(rates, pos, last):
    return jnp.exp(-rates * (pos.shape[1] - 1.0 - pos)) * last


def own_lanes(shape, group):
    lane = lax.broadcasted_iota(jnp.int32, shape, 1)
    return (lane >= group * GSIZE) & (lane < (group + 1) * GSIZE)


def weighted_state(rows, x, modes):
    hi, lo = split(rows)
    full = jnp.dot(hi, x, preferred_element_type=F32) + jnp.dot(lo, x, preferred_element_type=F32)
    state = jnp.zeros((modes, LANES), F32)
    for g in range(TILE_GROUPS):
        part = full[g * modes : (g + 1) * modes]
        state = jnp.where(own_lanes(part.shape, g), part, state)
    return state


def contract_first(a, b):
    return lax.dot_general(a, b, (((0,), (0,)), ((), ())), preferred_element_type=F32)


def from_state(rows, state, modes):
    blocks = [jnp.where(own_lanes(state.shape, g), state, 0.0) for g in range(TILE_GROUPS)]
    state_rows = jnp.concatenate(blocks, axis=0)
    r_hi, r_lo = split(rows)
    s_hi, s_lo = split(state_rows)
    return contract_first(r_hi, s_hi) + contract_first(r_lo, s_hi) + contract_first(r_hi, s_lo)


def convolve(left, right, mask, x, modes):
    l_hi, l_lo = split(left)
    r_hi, r_lo = split(right)
    total = jnp.zeros(x.shape, F32)
    for g in range(TILE_GROUPS):
        rows = slice(g * modes, (g + 1) * modes)
        a = jnp.concatenate([l_hi[rows], l_lo[rows], l_hi[rows]], axis=0)
        b = jnp.concatenate([r_hi[rows], r_hi[rows], r_lo[rows]], axis=0)
        kernel = (contract_first(a, b) * mask).astype(BF16)
        own = jnp.where(own_lanes(x.shape, g), x, jnp.zeros_like(x))
        total = total + jnp.dot(kernel, own, preferred_element_type=F32)
    return total


def when(cond):
    return pl.when(cond)


def fused(sizes, query, key, value, cot, w_hbm, rates, coeffs, skip, through, opened, first, last, mask, mask_t,
          yout, qgrad, kgrad, vgrad,
          w, wg, dyg, part, sbuf, rbuf, xg, yas, yar, ybs, ybr, yp, yf, yfs, yfr, acc, mixed, fgrad, fown, fin, bown, bin_,
          lsem, wss, wrs, css, crs, gss, grs, fss, frs, xss, xrs, dss, drs, ass, ars, bss, brs, yss, yrs,
          sfs, sfr, sbs, sbr):
    nz, nx, ny, hops, modes = sizes
    length, channels = query.shape
    width = w.shape[1]
    ctx = nz * nx
    rows = TILE_GROUPS * modes
    ring = part.shape[0]
    tiles = COLS // LANES
    nk = channels // COLS
    nw = width // COLS
    halves = 2
    hrows = length // halves
    z, x = lax.axis_index("z"), lax.axis_index("x")
    y, c = lax.axis_index("y"), lax.axis_index("c")
    t = y * CORES + c
    across = (t, x, lax.div(z, CORES), lax.rem(z, CORES))
    twin = (z, x, y, 1 - c)
    index = z * nx + x

    def along(move):
        return (lax.div(index + move, nx), lax.rem(index + move, nx), y, c)

    def cp(src, dst, ssem, rsem, dev):
        return pltpu.make_async_remote_copy(
            src_ref=src, dst_ref=dst, send_sem=ssem, recv_sem=rsem, device_id=dev, device_id_type=MESH
        )

    def cols(i):
        return pl.ds(pl.multiple_of(i * COLS, COLS), COLS)

    barrier = pltpu.get_barrier_semaphore()
    for dx in range(1, nx):
        pl.semaphore_signal(barrier, 1, device_id=(z, lax.rem(x + dx, nx), y, c), device_id_type=MESH)
    for dy in range(1, ny):
        pl.semaphore_signal(barrier, 1, device_id=(z, x, lax.rem(y + dy, ny), c), device_id_type=MESH)
    pl.semaphore_signal(barrier, 1, device_id=twin, device_id_type=MESH)

    @when(z > 0)
    def _():
        pl.semaphore_signal(barrier, 1, device_id=(z - 1, x, y, c), device_id_type=MESH)

    @when(z < nz - 1)
    def _():
        pl.semaphore_signal(barrier, 1, device_id=(z + 1, x, y, c), device_id_type=MESH)

    @when(t != z)
    def _():
        pl.semaphore_signal(barrier, 1, device_id=across, device_id_type=MESH)

    def one(cond):
        return cond.astype(jnp.int32)

    greetings = (nx - 1) + (ny - 1) + 1 + one(z > 0) + one(z < nz - 1) + one(t != z)
    for hop in range(1, hops + 1):
        for move in (hop, -hop):
            there = (index + move >= 0) & (index + move < ctx)
            greetings = greetings + one(there)

            @when(there)
            def _():
                pl.semaphore_signal(barrier, 1, device_id=along(move), device_id_type=MESH)

    pl.semaphore_wait(barrier, greetings)

    def w_copy(d, k):
        return cp(w_hbm.at[cols(k)], wg.at[d - 1, cols(k)], wss.at[d - 1, k], wrs.at[d - 1, k], (z, lax.rem(x + d, nx), y, c))

    def half(h):
        return pl.ds(h * hrows, hrows)

    def cot_copy(h):
        return cp(cot.at[half(h)], dyg.at[z, half(h)], css.at[h], crs.at[h], across)

    def cot_arrival(h):
        return cp(cot.at[half(h)], dyg.at[t, half(h)], css.at[h], crs.at[h], across)

    def spread(d, h):
        dev = twin if d == 0 else (z, x, lax.rem(y + d, ny), c)
        return cp(dyg.at[t, half(h)], dyg.at[t, half(h)], gss.at[d, h], grs.at[d, h], dev)

    def spread_arrival(d, h):
        slot = y * CORES + 1 - c if d == 0 else lax.rem(y + ny - d, ny) * CORES + c
        return slot, cp(dyg.at[slot, half(h)], dyg.at[slot, half(h)], gss.at[d, h], grs.at[d, h], twin)

    def relay(d, h):
        slot = lax.rem(y + ny - d, ny) * CORES + c
        return cp(dyg.at[slot, half(h)], dyg.at[slot, half(h)], fss.at[d - 1, h], frs.at[d - 1, h], twin)

    def relay_arrival(d, h):
        slot = lax.rem(y + ny - d, ny) * CORES + 1 - c
        return cp(dyg.at[slot, half(h)], dyg.at[slot, half(h)], fss.at[d - 1, h], frs.at[d - 1, h], twin)

    def x_copy(up, o, j):
        dev = (z + 1, x, y, c) if up else (z - 1, x, y, c)
        side = 0 if up else 1
        return cp(xg.at[o, :, cols(j)], xg.at[o, :, cols(j)], xss.at[side, o, j], xrs.at[o, j], dev)

    def d_copy(up, o, k):
        dev = (z + 1, x, y, c) if up else (z - 1, x, y, c)
        slot = o + 1 if up else o
        return cp(sbuf.at[o, k], rbuf.at[slot, k], dss.at[o, k], drs.at[slot, k], dev)

    def a_copy(o, q):
        slot = lax.div(o, CORES)
        return cp(yas.at[slot, :, cols(q)], yar.at[slot, :, cols(q)], ass.at[slot, q], ars.at[slot, q], twin)

    def b_copy(yd, q):
        slot = lax.rem(yd + ny - y, ny) - 1
        return cp(ybs.at[slot, :, cols(q)], ybr.at[slot, :, cols(q)], bss.at[slot, q], brs.at[slot, q], (z, x, yd, c))

    def y_copy(q):
        return cp(yfs.at[:, cols(q)], yfr.at[:, cols(q)], yss.at[q], yrs.at[q], across)

    def f_copy(hop, j):
        return cp(fown.at[j], fin.at[hop - 1, j], sfs.at[hop - 1, j], sfr.at[hop - 1, j], along(hop))

    def s_copy(hop, j):
        return cp(bown.at[j], bin_.at[hop - 1, j], sbs.at[hop - 1, j], sbr.at[hop - 1, j], along(-hop))

    pos = positions(rows, length)

    def lanes(j, i):
        return pl.ds(pl.multiple_of(j * COLS + i * LANES, LANES), LANES)

    def parameters(ref, j, i):
        tile = ref[pl.ds(pl.multiple_of((j * tiles + i) * rows, rows), rows), :]
        return jnp.concatenate([tile] * (length // LANES), axis=1)

    def gated_of(at):
        return (key[:, at].astype(F32) * value[:, at].astype(F32)).astype(BF16)

    def forward_state(j):
        for i in range(tiles):
            r = parameters(rates, j, i)
            fown[j, :, i * LANES : (i + 1) * LANES] = weighted_state(
                outflow_rows(r, pos, last[...]), gated_of(lanes(j, i)), modes
            )
        for hop in range(1, hops + 1):
            @when(index + hop < ctx)
            def _():
                f_copy(hop, j).start()

    def entering(j, copy, ref, sign, way):
        acc[:modes, :] = jnp.zeros((modes, COLS), F32)
        factor = jnp.ones((modes, COLS), F32)
        for hop in range(1, hops + 1):
            there = (index - hop >= 0) if sign > 0 else (index + hop < ctx)
            now = factor

            @when(there)
            def _():
                copy(hop, j).wait_recv()
                acc[:modes, :] += now * ref[hop - 1, j]

            row = opened[way * hops + hop - 1 : way * hops + hop, :]
            factor = factor * through[:, cols(j)] * jnp.concatenate([row] * tiles, axis=1)

    def forward_filter(j):
        entering(j, f_copy, fin, 1, 0)
        for i in range(tiles):
            at = lanes(j, i)
            r, co = parameters(rates, j, i), parameters(coeffs, j, i)
            g = gated_of(at)
            half = length / 2.0
            total = convolve(co * jnp.exp(-r * (pos - half)), jnp.exp(r * (pos - half)), mask[...], g, modes)
            total = total + from_state(
                inflow_rows(r, co, pos, first[...]), acc[:modes, i * LANES : (i + 1) * LANES], modes
            )
            result = total.astype(BF16).astype(F32) + skip[:, at] * g.astype(F32)
            mixed[:, at] = result
            xg[z, :, at] = (query[:, at].astype(F32) * result).astype(BF16)

        @when(z < nz - 1)
        def _():
            x_copy(True, z, j).start()

        @when(z > 0)
        def _():
            x_copy(False, z, j).start()

    def adjoint_state(j):
        for i in range(tiles):
            at = lanes(j, i)
            r, co = parameters(rates, j, i), parameters(coeffs, j, i)
            g = acc[:, i * LANES : (i + 1) * LANES].astype(BF16).astype(F32)
            f = (g * query[:, at].astype(F32)).astype(BF16)
            fgrad[:, at] = f
            qgrad[:, at] = (g * mixed[:, at]).astype(BF16)
            bown[j, :, i * LANES : (i + 1) * LANES] = weighted_state(inflow_rows(r, co, pos, first[...]), f, modes)
        for hop in range(1, hops + 1):
            @when(index - hop >= 0)
            def _():
                s_copy(hop, j).start()

    def adjoint_filter(j):
        entering(j, s_copy, bin_, -1, 1)
        for i in range(tiles):
            at = lanes(j, i)
            r, co = parameters(rates, j, i), parameters(coeffs, j, i)
            f = fgrad[:, at]
            half = length / 2.0
            total = convolve(jnp.exp(r * (pos - half)), co * jnp.exp(-r * (pos - half)), mask_t[...], f, modes)
            total = total + from_state(
                outflow_rows(r, pos, last[...]), acc[:modes, i * LANES : (i + 1) * LANES], modes
            )
            result = total.astype(BF16).astype(F32) + skip[:, at] * f.astype(F32)
            kgrad[:, at] = (result * value[:, at].astype(F32)).astype(BF16)
            vgrad[:, at] = (result * key[:, at].astype(F32)).astype(BF16)

    @when(t != z)
    def _():
        for h in range(halves):
            cot_copy(h).start()

    own_cot = pltpu.make_async_copy(cot, dyg.at[z], lsem.at[1])

    @when(t == z)
    def _():
        own_cot.start()

    def start_w(k, _):
        for d in range(1, nx):
            w_copy(d, k).start()
        return 0

    lax.fori_loop(0, nk, start_w, 0)
    own_w = pltpu.make_async_copy(w_hbm, w, lsem.at[0])
    own_w.start()

    def repeat(lo, hi, body):
        def run(j, _):
            body(j)
            return 0

        lax.fori_loop(lo, hi, run, 0)

    repeat(0, nk, forward_state)
    repeat(0, nk // 2, forward_filter)

    @when(t == z)
    def _():
        own_cot.wait()

    for h in range(halves):
        @when(t != z)
        def _():
            cot_arrival(h).wait_recv()

        for d in range(ny):
            spread(d, h).start()

    repeat(nk // 2, nk, forward_filter)

    for h in range(halves):
        for d in range(1, ny):
            spread_arrival(d, h)[1].wait_recv()
            relay(d, h).start()
    own_w.wait()
    for h in range(halves):
        spread_arrival(0, h)[1].wait_recv()
        for d in range(1, ny):
            relay_arrival(d, h).wait_recv()

    def valid(k):
        return (k >= 0) & (k < nk)

    lag = jnp.maximum(z, nz - 1 - z)

    def block(o):
        slot = lax.div(o, CORES)
        core, yd = lax.rem(o, CORES), lax.div(o, CORES)

        for src in range(nx):
            def column(i, _):
                q = lax.rem(x + nx - src, nx) * nw + i
                ref = w if src == 0 else wg.at[src - 1]
                p = jnp.dot(xg[o], ref[:, cols(i)], preferred_element_type=F32)

                @when(c != core)
                def _():
                    yas[slot, :, cols(q)] = p.astype(BF16)
                    a_copy(o, q).start()

                @when(c == core)
                def _():
                    yp[:, cols(q)] = p

                return 0

            lax.fori_loop(0, nw, column, 0)

        @when(c == core)
        def _():
            def add(i, _):
                q = lax.rem(x * nw + i, nk)
                a_copy(o, q).wait_recv()
                total = yp[:, cols(q)] + yar[slot, :, cols(q)].astype(F32)

                @when(yd != y)
                def _():
                    ybs[lax.rem(yd + ny - y, ny) - 1, :, cols(q)] = total.astype(BF16)
                    b_copy(yd, q).start()

                @when(yd == y)
                def _():
                    yf[:, cols(q)] = total

                return 0

            lax.fori_loop(0, nk, add, 0)

    def finish():
        def one(i, _):
            q = lax.rem(x * nw + i, nk)
            total = yf[:, cols(q)]
            for d in range(1, ny):
                cp(ybs.at[d - 1, :, cols(q)], ybr.at[d - 1, :, cols(q)], bss.at[d - 1, q], brs.at[d - 1, q], twin).wait_recv()
                total = total + ybr[d - 1, :, cols(q)].astype(F32)

            yfs[:, cols(q)] = total.astype(BF16)

            @when(t != z)
            def _():
                y_copy(q).start()

            return 0

        lax.fori_loop(0, nk, one, 0)

    def step(s, _):
        for h in range(1, nz):
            j = s - (h - 1)
            for up in (True, False):
                o = z - h if up else z + h
                there = (o >= 0) if up else (o < nz)
                further = (z < nz - 1) if up else (z > 0)

                @when(valid(j) & there)
                def _():
                    x_copy(up, o, j).wait_recv()

                    @when(further)
                    def _():
                        x_copy(up, o, j).start()

        @when(s < nk)
        def _():
            for d in range(1, nx):
                w_copy(d, s).wait_recv()
            own_cols = pl.ds(pl.multiple_of(x * width, LANES), width)

            def rows_of(o, _):
                total = lax.dot_general(
                    dyg[o, :, own_cols], w[cols(s), :], (((1,), (1,)), ((), ())), preferred_element_type=F32
                )
                for d in range(1, nx):
                    from_cols = pl.ds(pl.multiple_of(lax.rem(x + nx - d, nx) * width, LANES), width)
                    total = total + lax.dot_general(
                        dyg[o, :, from_cols], wg[d - 1, cols(s), :], (((1,), (1,)), ((), ())), preferred_element_type=F32
                    )
                part[lax.rem(s, ring), o] = total
                return 0

            lax.fori_loop(0, nz, rows_of, 0)

        up_k = s - z

        @when(valid(up_k) & (z < nz - 1))
        def _():
            for o in range(nz - 1, 0, -1):
                @when(o > z)
                def _():
                    @when(z > 0)
                    def _():
                        d_copy(True, o, up_k).wait_recv()
                        sbuf[o, up_k] = (part[lax.rem(up_k, ring), o] + rbuf[o + 1, up_k].astype(F32)).astype(BF16)

                    @when(z == 0)
                    def _():
                        sbuf[o, up_k] = part[lax.rem(up_k, ring), o].astype(BF16)

                    d_copy(True, o, up_k).start()

        down_k = s - (nz - 1 - z)

        @when(valid(down_k) & (z > 0))
        def _():
            for o in range(nz - 1):
                @when(o < z)
                def _():
                    @when(z < nz - 1)
                    def _():
                        d_copy(False, o, down_k).wait_recv()
                        sbuf[o, down_k] = (part[lax.rem(down_k, ring), o] + rbuf[o, down_k].astype(F32)).astype(BF16)

                    @when(z == nz - 1)
                    def _():
                        sbuf[o, down_k] = part[lax.rem(down_k, ring), o].astype(BF16)

                    d_copy(False, o, down_k).start()

        own_k = s - lag

        @when(valid(own_k))
        def _():
            acc[...] = part[lax.rem(own_k, ring), z]

            @when(z > 0)
            def _():
                d_copy(True, z, own_k).wait_recv()
                acc[...] += rbuf[z + 1, own_k].astype(F32)

            @when(z < nz - 1)
            def _():
                d_copy(False, z, own_k).wait_recv()
                acc[...] += rbuf[z, own_k].astype(F32)

            adjoint_state(own_k)

        far_k = s - nz

        @when(valid(far_k))
        def _():
            adjoint_filter(far_k)

        h = s - nk

        @when((h >= 0) & (h < nz))
        def _():
            @when(z + h < nz)
            def _():
                block(z + h)

            @when((h > 0) & (z - h >= 0))
            def _():
                block(z - h)

            @when((h > 0) & ((t - z == h - 1) | (z - t == h - 1)))
            def _():
                finish()

        return 0

    lax.fori_loop(0, nk + nz, step, 0)

    @when((t - z == nz - 1) | (z - t == nz - 1))
    def _():
        finish()

    @when(t == z)
    def _():
        yout[...] = yfs[...]

    @when(t != z)
    def _():
        def land(q, _):
            y_copy(q).wait()
            return 0

        lax.fori_loop(0, nk, land, 0)
        yout[...] = yfr[...]
        for h in range(halves):
            cot_copy(h).wait_send()

    for h in range(halves):
        for d in range(ny):
            spread(d, h).wait_send()
        for d in range(1, ny):
            relay(d, h).wait_send()

    def drain(k, _):
        for d in range(1, nx):
            w_copy(d, k).wait_send()
        for slot in range(ny):
            a_copy(slot * CORES + 1 - c, k).wait_send()
        for d in range(1, ny):
            b_copy(lax.rem(y + d, ny), k).wait_send()
        for o in range(nz):
            @when((z < nz - 1) & (o <= z))
            def _():
                x_copy(True, o, k).wait_send()

            @when((z > 0) & (o >= z))
            def _():
                x_copy(False, o, k).wait_send()

            @when(o > z)
            def _():
                d_copy(True, o, k).wait_send()

            @when(o < z)
            def _():
                d_copy(False, o, k).wait_send()

        for hop in range(1, hops + 1):
            @when(index + hop < ctx)
            def _():
                f_copy(hop, k).wait_send()

            @when(index - hop >= 0)
            def _():
                s_copy(hop, k).wait_send()

        return 0

    lax.fori_loop(0, nk, drain, 0)


def fused_call(sizes, tokens, cot, weight, parameters):
    nz, nx, ny, hops, modes = sizes
    length, channels = cot.shape
    width = weight.shape[1]
    nk = channels // COLS
    vmem = pl.BlockSpec(memory_space=pltpu.VMEM)
    hbm = pl.BlockSpec(memory_space=pl.ANY)
    token = jax.ShapeDtypeStruct((length, channels), BF16)
    dma = pltpu.SemaphoreType.DMA
    near = max(ny - 1, 1)
    wide_x = max(nx - 1, 1)
    flops = 8 * nz * length * channels * width * nx // 2
    return pl.pallas_call(
        functools.partial(fused, sizes),
        out_shape=(token,) * 4,
        in_specs=[vmem] * 3 + [hbm] * 2 + [vmem] * len(parameters),
        out_specs=(vmem,) * 4,
        scratch_shapes=[
            pltpu.VMEM((channels, width), BF16),
            pltpu.VMEM((wide_x, channels, width), BF16),
            pltpu.VMEM((nz, length, channels), BF16),
            pltpu.VMEM((nz, nz, length, COLS), F32),
            pltpu.VMEM((nz, nk, length, COLS), BF16),
            pltpu.VMEM((nz + 1, nk, length, COLS), BF16),
            pltpu.VMEM((nz, length, channels), BF16),
            pltpu.VMEM((ny, length, channels), BF16),
            pltpu.VMEM((ny, length, channels), BF16),
            pltpu.VMEM((near, length, channels), BF16),
            pltpu.VMEM((near, length, channels), BF16),
            pltpu.VMEM((length, channels), F32),
            pltpu.VMEM((length, channels), F32),
            pltpu.VMEM((length, channels), BF16),
            pltpu.VMEM((length, channels), BF16),
            pltpu.VMEM((length, COLS), F32),
            pltpu.VMEM((length, channels), F32),
            pltpu.VMEM((length, channels), BF16),
            pltpu.VMEM((nk, modes, COLS), F32),
            pltpu.VMEM((hops, nk, modes, COLS), F32),
            pltpu.VMEM((nk, modes, COLS), F32),
            pltpu.VMEM((hops, nk, modes, COLS), F32),
            dma((2,)),
            dma((wide_x, nk)), dma((wide_x, nk)),
            dma((2,)), dma((2,)),
            dma((ny, 2)), dma((ny, 2)),
            dma((near, 2)), dma((near, 2)),
            dma((2, nz, nk)), dma((nz, nk)),
            dma((nz, nk)), dma((nz + 1, nk)),
            dma((ny, nk)), dma((ny, nk)),
            dma((near, nk)), dma((near, nk)),
            dma((nk,)), dma((nk,)),
            dma((hops, nk)), dma((hops, nk)),
            dma((hops, nk)), dma((hops, nk)),
        ],
        compiler_params=pltpu.CompilerParams(
            collective_id=0, has_side_effects=True, vmem_limit_bytes=63 * 2**20
        ),
        cost_estimate=pl.CostEstimate(flops=flops, bytes_accessed=16 * 2**20, transcendentals=0),
    )(*tokens, cot, weight, *parameters)


def on_device(
    query_branch,
    key_branch,
    value_branch,
    out_cotangent,
    out_weight,
    residues,
    decay_rates,
    skip_gains,
    record_lengths,
):
    length, channels = query_branch.shape
    modes = residues.shape[1]
    nz, nx, ny = lax.axis_size("z"), lax.axis_size("x"), lax.axis_size("y")
    ctx = nz * nx
    hops = -(-(length * ctx // 4) // length)
    index = lax.axis_index("z") * nx + lax.axis_index("x")

    records = record_lengths.shape[0]
    before = jnp.arange(records)[:, None] > jnp.arange(records)[None, :]
    offsets = jnp.sum(jnp.where(before, record_lengths[None, :], 0), axis=1)
    blocks = jnp.arange(ctx, dtype=jnp.int32) * length
    closed = jnp.any(
        (offsets[None, :] >= blocks[:, None]) & (offsets[None, :] < blocks[:, None] + length), axis=1
    ).astype(jnp.int32)
    at = jnp.arange(length, dtype=jnp.int32)
    local = offsets - index * length

    def segment_of(pos):
        shape = (1,) * pos.ndim
        starts = local.reshape((-1,) + shape)
        return jnp.sum(((starts >= 0) & (starts <= pos[None])).astype(jnp.int32), axis=0)

    segment = segment_of(at)
    final = jnp.sum(((local >= 0) & (local < length)).astype(jnp.int32))
    first = (segment == 0).astype(F32)[None, :]
    last = (segment == final).astype(F32)[None, :]
    mask = ((at[:, None] >= at[None, :]) & (segment[:, None] == segment[None, :])).astype(F32)

    coeffs = residues * jnp.sqrt(1.0 - jnp.exp(-2.0 * decay_rates))
    rates_rows = jnp.broadcast_to(decay_rates.reshape(-1, 1), (decay_rates.size, LANES))
    coeff_rows = jnp.broadcast_to(coeffs.reshape(-1, 1), (coeffs.size, LANES))
    through = jnp.repeat(jnp.exp(-decay_rates * length).T, GSIZE, axis=1)
    skip = skip_gains[None, :]
    def opened(direction):
        passed = jnp.clip(index - direction * (1 + jnp.arange(hops)), 0, ctx - 1)
        return jnp.broadcast_to((1.0 - closed[passed].astype(F32))[:, None], (hops, LANES))

    doors = jnp.concatenate([opened(1), opened(-1)], axis=0)
    return fused_call(
        (nz, nx, ny, hops, modes),
        (query_branch, key_branch, value_branch), out_cotangent, out_weight,
        (rates_rows, coeff_rows, skip, through, doors, first, last, mask, mask.T),
    )


def solution(mesh):
    ctx, tp = mesh.devices.shape
    fine = Mesh(mesh.devices.reshape(tp, ctx // tp, tp // CORES, CORES), ("z", "x", "y", "c"))
    tokens = P(("z", "x"), ("y", "c"))
    placed = (
        tokens,
        tokens,
        tokens,
        tokens,
        P(("y", "c"), ("z", "x")),
        P(("y", "c"), None),
        P(("y", "c"), None),
        P(("y", "c")),
        P(),
    )
    return jax.shard_map(
        on_device,
        mesh=fine,
        in_specs=placed,
        out_specs=(tokens, tokens, tokens, tokens),
        check_vma=False,
    )
```

```python
import functools

import jax
import jax.numpy as jnp
from jax import lax
from jax.experimental import pallas as pl
from jax.experimental.pallas import tpu as pltpu
from jax.sharding import Mesh, PartitionSpec as P

GSIZE = 16
LANES = 128
TILE_GROUPS = LANES // GSIZE
CORES = 2
COLS = 256
PIECES = 4
AHEAD = 4
F32, BF16 = jnp.float32, jnp.bfloat16
MESH = pl.DeviceIdType.MESH


def split(a):
    hi = a.astype(BF16)
    return hi, (a - hi.astype(F32)).astype(BF16)


def positions(rows, length):
    return lax.broadcasted_iota(jnp.int32, (rows, length), 1).astype(F32)


def inflow_rows(rates, coeffs, pos, first):
    return coeffs * jnp.exp(-rates * (pos + 1.0)) * first


def outflow_rows(rates, pos, last):
    return jnp.exp(-rates * (pos.shape[1] - 1.0 - pos)) * last


def own_lanes(shape, group):
    lane = lax.broadcasted_iota(jnp.int32, shape, 1)
    return (lane >= group * GSIZE) & (lane < (group + 1) * GSIZE)


def weighted_state(rows, x, modes):
    hi, lo = split(rows)
    full = jnp.dot(hi, x, preferred_element_type=F32) + jnp.dot(lo, x, preferred_element_type=F32)
    state = jnp.zeros((modes, LANES), F32)
    for g in range(TILE_GROUPS):
        part = full[g * modes : (g + 1) * modes]
        state = jnp.where(own_lanes(part.shape, g), part, state)
    return state


def contract_first(a, b):
    return lax.dot_general(a, b, (((0,), (0,)), ((), ())), preferred_element_type=F32)


def from_state(rows, state, modes):
    blocks = [jnp.where(own_lanes(state.shape, g), state, 0.0) for g in range(TILE_GROUPS)]
    state_rows = jnp.concatenate(blocks, axis=0)
    r_hi, r_lo = split(rows)
    s_hi, s_lo = split(state_rows)
    return contract_first(r_hi, s_hi) + contract_first(r_lo, s_hi) + contract_first(r_hi, s_lo)


def convolve(left, right, mask, x, modes):
    l_hi, l_lo = split(left)
    r_hi, r_lo = split(right)
    total = jnp.zeros(x.shape, F32)
    for g in range(TILE_GROUPS):
        rows = slice(g * modes, (g + 1) * modes)
        a = jnp.concatenate([l_hi[rows], l_lo[rows], l_hi[rows]], axis=0)
        b = jnp.concatenate([r_hi[rows], r_hi[rows], r_lo[rows]], axis=0)
        kernel = (contract_first(a, b) * mask).astype(BF16)
        own = jnp.where(own_lanes(x.shape, g), x, jnp.zeros_like(x))
        total = total + jnp.dot(kernel, own, preferred_element_type=F32)
    return total


def when(cond):
    return pl.when(cond)


def fused(sizes, query, key, value, cot, w_hbm, rates, coeffs, skip, through, opened, first, last, mask, mask_t,
          yout, qgrad, kgrad, vgrad,
          w, wg, dyg, part, sbuf, rbuf, xg, yas, yar, ybs, ybr, yp, yf, yfs, yfr, acc, mixed, fgrad, fown, fin, bown, bin_, crelay,
          lsem, rss, rrs, wss, wrs, css, crs, gss, grs, fss, frs, xss, xrs, dss, drs, ass, ars, bss, brs, yss, yrs,
          sfs, sfr, sbs, sbr):
    nz, nx, ny, hops, modes = sizes
    length, channels = query.shape
    width = w.shape[1]
    ctx = nz * nx
    rows = TILE_GROUPS * modes
    ring = part.shape[0]
    tiles = COLS // LANES
    nk = channels // COLS
    nw = width // COLS
    halves = PIECES
    hrows = length // halves
    z, x = lax.axis_index("z"), lax.axis_index("x")
    y, c = lax.axis_index("y"), lax.axis_index("c")
    t = y * CORES + c
    mine = c * ny + lax.rem(y - z + nz * ny, ny)
    holder = (t, x, lax.rem(z + t, ny), lax.div(z, ny))
    owner = (mine, x, lax.div(z, CORES), lax.rem(z, CORES))
    stays = (t == z) & (y == lax.rem(z + t, ny)) & (c == lax.div(z, ny))
    leaves = jnp.logical_not(stays)
    two_lines = ny == 2
    on_line = y == lax.rem(z + c, ny)
    via = (z, x, lax.rem(y + 1, ny), c)
    side_t = lax.rem(y + 1, ny) * CORES + c
    side_holder = (side_t, x, y, lax.div(z, ny))
    side_stays = on_line & (side_t == z) & (c == lax.div(z, ny))
    side_leaves = on_line & jnp.logical_not(side_stays)
    side_source = (mine, x, y, lax.rem(z, CORES))
    by_side = (y != lax.div(z, CORES)) & jnp.logical_not((mine == z) & (c == lax.rem(z, CORES)))
    if not two_lines:
        on_line = y == y
        side_stays = side_leaves = by_side = y != y
    arrives = leaves & jnp.logical_not(side_stays)
    twin = (z, x, y, 1 - c)
    index = z * nx + x

    def along(move):
        return (lax.div(index + move, nx), lax.rem(index + move, nx), y, c)

    def cp(src, dst, ssem, rsem, dev):
        return pltpu.make_async_remote_copy(
            src_ref=src, dst_ref=dst, send_sem=ssem, recv_sem=rsem, device_id=dev, device_id_type=MESH
        )

    def cols(i):
        return pl.ds(pl.multiple_of(i * COLS, COLS), COLS)

    barrier = pltpu.get_barrier_semaphore()
    for dx in range(1, nx):
        pl.semaphore_signal(barrier, 1, device_id=(z, lax.rem(x + dx, nx), y, c), device_id_type=MESH)
    for dy in range(1, ny):
        pl.semaphore_signal(barrier, 1, device_id=(z, x, lax.rem(y + dy, ny), c), device_id_type=MESH)
    pl.semaphore_signal(barrier, 1, device_id=twin, device_id_type=MESH)

    @when(z > 0)
    def _():
        pl.semaphore_signal(barrier, 1, device_id=(z - 1, x, y, c), device_id_type=MESH)

    @when(z < nz - 1)
    def _():
        pl.semaphore_signal(barrier, 1, device_id=(z + 1, x, y, c), device_id_type=MESH)

    @when(leaves)
    def _():
        pl.semaphore_signal(barrier, 1, device_id=holder, device_id_type=MESH)
        pl.semaphore_signal(barrier, 1, device_id=owner, device_id_type=MESH)

    @when(side_leaves)
    def _():
        pl.semaphore_signal(barrier, 1, device_id=side_holder, device_id_type=MESH)

    @when(by_side)
    def _():
        pl.semaphore_signal(barrier, 1, device_id=side_source, device_id_type=MESH)

    def one(cond):
        return cond.astype(jnp.int32)

    greetings = (nx - 1) + (ny - 1) + 1 + one(z > 0) + one(z < nz - 1) + 2 * one(leaves) + one(side_leaves) + one(by_side)
    for hop in range(1, hops + 1):
        for move in (hop, -hop):
            there = (index + move >= 0) & (index + move < ctx)
            greetings = greetings + one(there)

            @when(there)
            def _():
                pl.semaphore_signal(barrier, 1, device_id=along(move), device_id_type=MESH)

    pl.semaphore_wait(barrier, greetings)

    def w_copy(d, k):
        return cp(w_hbm.at[cols(k)], wg.at[d - 1, cols(k)], wss.at[d - 1, k], wrs.at[d - 1, k], (z, lax.rem(x + d, nx), y, c))

    def half(h):
        return pl.ds(h * hrows, hrows)

    def cot_copy(h):
        return cp(cot.at[half(h)], dyg.at[z, half(h)], css.at[h], crs.at[h], holder)

    def side_copy(h):
        return cp(cot.at[half(h)], crelay.at[half(h)], rss.at[h], rrs.at[h], via)

    def side_relay(h):
        return cp(crelay.at[half(h)], dyg.at[z, half(h)], rss.at[h], crs.at[h], side_holder)

    def cot_arrival(h):
        return cp(cot.at[half(h)], dyg.at[mine, half(h)], css.at[h], crs.at[h], holder)

    def held_by(core, d):
        return core * ny + lax.rem(y - d - z + nz * ny + ny, ny)

    def spread(d, h):
        dev = twin if d == 0 else (z, x, lax.rem(y + d, ny), c)
        return cp(dyg.at[mine, half(h)], dyg.at[mine, half(h)], gss.at[d, h], grs.at[d, h], dev)

    def spread_arrival(d, h):
        slot = held_by(1 - c if d == 0 else c, d)
        return cp(dyg.at[slot, half(h)], dyg.at[slot, half(h)], gss.at[d, h], grs.at[d, h], twin)

    def relay(d, h):
        slot = held_by(c, d)
        return cp(dyg.at[slot, half(h)], dyg.at[slot, half(h)], fss.at[d - 1, h], frs.at[d - 1, h], twin)

    def relay_arrival(d, h):
        slot = held_by(1 - c, d)
        return cp(dyg.at[slot, half(h)], dyg.at[slot, half(h)], fss.at[d - 1, h], frs.at[d - 1, h], twin)

    def x_copy(up, o, j):
        dev = (z + 1, x, y, c) if up else (z - 1, x, y, c)
        side = 0 if up else 1
        return cp(xg.at[o, :, cols(j)], xg.at[o, :, cols(j)], xss.at[side, o, j], xrs.at[o, j], dev)

    def d_copy(up, o, k):
        dev = (z + 1, x, y, c) if up else (z - 1, x, y, c)
        slot = o + 1 if up else o
        return cp(sbuf.at[o, k], rbuf.at[slot, k], dss.at[o, k], drs.at[slot, k], dev)

    def a_copy(o, q):
        slot = lax.rem(o, ny)
        return cp(yas.at[slot, :, cols(q)], yar.at[slot, :, cols(q)], ass.at[slot, q], ars.at[slot, q], twin)

    def b_copy(yd, q):
        slot = lax.rem(yd + ny - y, ny) - 1
        return cp(ybs.at[slot, :, cols(q)], ybr.at[slot, :, cols(q)], bss.at[slot, q], brs.at[slot, q], (z, x, yd, c))

    def y_copy(q):
        return cp(yfs.at[:, cols(q)], yfr.at[:, cols(q)], yss.at[q], yrs.at[q], owner)

    def f_copy(hop, j):
        return cp(fown.at[j], fin.at[hop - 1, j], sfs.at[hop - 1, j], sfr.at[hop - 1, j], along(hop))

    def s_copy(hop, j):
        return cp(bown.at[j], bin_.at[hop - 1, j], sbs.at[hop - 1, j], sbr.at[hop - 1, j], along(-hop))

    pos = positions(rows, length)

    def lanes(j, i):
        return pl.ds(pl.multiple_of(j * COLS + i * LANES, LANES), LANES)

    def parameters(ref, j, i):
        tile = ref[pl.ds(pl.multiple_of((j * tiles + i) * rows, rows), rows), :]
        return jnp.concatenate([tile] * (length // LANES), axis=1)

    def gated_of(at):
        return (key[:, at].astype(F32) * value[:, at].astype(F32)).astype(BF16)

    def forward_state(j):
        for i in range(tiles):
            r = parameters(rates, j, i)
            fown[j, :, i * LANES : (i + 1) * LANES] = weighted_state(
                outflow_rows(r, pos, last[...]), gated_of(lanes(j, i)), modes
            )
        for hop in range(1, hops + 1):
            @when(index + hop < ctx)
            def _():
                f_copy(hop, j).start()

    def entering(j, copy, ref, sign, way):
        acc[:modes, :] = jnp.zeros((modes, COLS), F32)
        factor = jnp.ones((modes, COLS), F32)
        for hop in range(1, hops + 1):
            there = (index - hop >= 0) if sign > 0 else (index + hop < ctx)
            now = factor

            @when(there)
            def _():
                copy(hop, j).wait_recv()
                acc[:modes, :] += now * ref[hop - 1, j]

            row = opened[way * hops + hop - 1 : way * hops + hop, :]
            factor = factor * through[:, cols(j)] * jnp.concatenate([row] * tiles, axis=1)

    def forward_filter(j):
        entering(j, f_copy, fin, 1, 0)
        for i in range(tiles):
            at = lanes(j, i)
            r, co = parameters(rates, j, i), parameters(coeffs, j, i)
            g = gated_of(at)
            half = length / 2.0
            total = convolve(co * jnp.exp(-r * (pos - half)), jnp.exp(r * (pos - half)), mask[...], g, modes)
            total = total + from_state(
                inflow_rows(r, co, pos, first[...]), acc[:modes, i * LANES : (i + 1) * LANES], modes
            )
            result = total.astype(BF16).astype(F32) + skip[:, at] * g.astype(F32)
            mixed[:, at] = result
            xg[z, :, at] = (query[:, at].astype(F32) * result).astype(BF16)

        @when(z < nz - 1)
        def _():
            x_copy(True, z, j).start()

        @when(z > 0)
        def _():
            x_copy(False, z, j).start()

    def adjoint_state(j):
        for i in range(tiles):
            at = lanes(j, i)
            r, co = parameters(rates, j, i), parameters(coeffs, j, i)
            g = acc[:, i * LANES : (i + 1) * LANES].astype(BF16).astype(F32)
            f = (g * query[:, at].astype(F32)).astype(BF16)
            fgrad[:, at] = f
            qgrad[:, at] = (g * mixed[:, at]).astype(BF16)
            bown[j, :, i * LANES : (i + 1) * LANES] = weighted_state(inflow_rows(r, co, pos, first[...]), f, modes)
        for hop in range(1, hops + 1):
            @when(index - hop >= 0)
            def _():
                s_copy(hop, j).start()

    def adjoint_filter(j):
        entering(j, s_copy, bin_, -1, 1)
        for i in range(tiles):
            at = lanes(j, i)
            r, co = parameters(rates, j, i), parameters(coeffs, j, i)
            f = fgrad[:, at]
            half = length / 2.0
            total = convolve(jnp.exp(r * (pos - half)), co * jnp.exp(-r * (pos - half)), mask_t[...], f, modes)
            total = total + from_state(
                outflow_rows(r, pos, last[...]), acc[:modes, i * LANES : (i + 1) * LANES], modes
            )
            result = total.astype(BF16).astype(F32) + skip[:, at] * f.astype(F32)
            kgrad[:, at] = (result * value[:, at].astype(F32)).astype(BF16)
            vgrad[:, at] = (result * key[:, at].astype(F32)).astype(BF16)

    own_cot = pltpu.make_async_copy(cot, dyg.at[z], lsem.at[1])
    own_w = pltpu.make_async_copy(w_hbm, w, lsem.at[0])

    def start_w(k):
        for d in range(1, nx):
            w_copy(d, k).start()

    def repeat(lo, hi, body):
        def run(j, _):
            body(j)
            return 0

        lax.fori_loop(lo, hi, run, 0)

    def valid(k):
        return (k >= 0) & (k < nk)

    def pass_on(s):
        for h in range(1, nz):
            j = s - (h - 1)
            for up in (True, False):
                o = z - h if up else z + h
                there = (o >= 0) if up else (o < nz)
                further = (z < nz - 1) if up else (z > 0)

                @when(valid(j) & there)
                def _():
                    x_copy(up, o, j).wait_recv()

                    @when(further)
                    def _():
                        x_copy(up, o, j).start()

    repeat(0, nk, forward_state)

    @when(leaves & on_line)
    def _():
        for h in range(halves):
            cot_copy(h).start()

    @when(jnp.logical_not(on_line))
    def _():
        for h in range(halves):
            side_copy(h).start()

    @when(stays)
    def _():
        own_cot.start()

    repeat(0, nk, start_w)
    own_w.start()
    repeat(0, nk // 2, forward_filter)

    if two_lines:
        @when(on_line)
        def _():
            for h in range(halves):
                side_copy(h).wait_recv()

                @when(side_leaves)
                def _():
                    side_relay(h).start()

                @when(side_stays)
                def _():
                    dyg[z, half(h)] = crelay[half(h)]

    repeat(nk // 2, nk, forward_filter)
    repeat(0, AHEAD // 2, pass_on)

    @when(stays)
    def _():
        own_cot.wait()

    for h in range(halves):
        @when(arrives)
        def _():
            cot_arrival(h).wait_recv()

        for d in range(ny):
            spread(d, h).start()

    repeat(AHEAD // 2, AHEAD, pass_on)

    for h in range(halves):
        for d in range(1, ny):
            spread_arrival(d, h).wait_recv()
            relay(d, h).start()
    own_w.wait()
    for h in range(halves):
        spread_arrival(0, h).wait_recv()
        for d in range(1, ny):
            relay_arrival(d, h).wait_recv()

    lag = jnp.maximum(z, nz - 1 - z)

    def column_of(src, i):
        return lax.rem(x + nx - src, nx) * nw + i

    def block(src, o):
        slot, core = lax.rem(o, ny), lax.div(o, ny)
        yd = lax.rem(o + z, ny)

        def column(i, _):
            q = column_of(src, i)
            ref = w if src == 0 else wg.at[src - 1]
            p = jnp.dot(xg[o], ref[:, cols(i)], preferred_element_type=F32)

            @when(c != core)
            def _():
                yas[slot, :, cols(q)] = p.astype(BF16)
                a_copy(o, q).start()

            @when(c == core)
            def _():
                yp[:, cols(q)] = p

            return 0

        lax.fori_loop(0, nw, column, 0)

        @when(c == core)
        def _():
            def add(i, _):
                q = column_of(src, i)
                a_copy(o, q).wait_recv()
                total = yp[:, cols(q)] + yar[slot, :, cols(q)].astype(F32)

                @when(yd != y)
                def _():
                    ybs[lax.rem(yd + ny - y, ny) - 1, :, cols(q)] = total.astype(BF16)
                    b_copy(yd, q).start()

                @when(yd == y)
                def _():
                    yf[:, cols(q)] = total

                return 0

            lax.fori_loop(0, nw, add, 0)

    def blocks(src, h):
        def side(i, _):
            o = z + h * (1 - 2 * i)

            @when((o >= 0) & (o < nz) & ((h > 0) | (i == 0)))
            def _():
                block(src, o)

            return 0

        lax.fori_loop(0, 2, side, 0)

    def finish(src):
        def last_sum(i, _):
            q = column_of(src, i)
            total = yf[:, cols(q)]
            for d in range(1, ny):
                cp(ybs.at[d - 1, :, cols(q)], ybr.at[d - 1, :, cols(q)], bss.at[d - 1, q], brs.at[d - 1, q], twin).wait_recv()
                total = total + ybr[d - 1, :, cols(q)].astype(F32)

            yfs[:, cols(q)] = total.astype(BF16)

            @when(leaves)
            def _():
                y_copy(q).start()

            return 0

        lax.fori_loop(0, nw, last_sum, 0)

    distance = jnp.maximum(mine - z, z - mine)

    def step(s, _):
        pass_on(s)
        k = s - AHEAD

        @when(k < nk)
        def _():
            for d in range(1, nx):
                w_copy(d, k).wait_recv()
            own_cols = pl.ds(pl.multiple_of(x * width, LANES), width)

            def rows_of(o, _):
                total = lax.dot_general(
                    dyg[o, :, own_cols], w[cols(k), :], (((1,), (1,)), ((), ())), preferred_element_type=F32
                )
                for d in range(1, nx):
                    from_cols = pl.ds(pl.multiple_of(lax.rem(x + nx - d, nx) * width, LANES), width)
                    total = total + lax.dot_general(
                        dyg[o, :, from_cols], wg[d - 1, cols(k), :], (((1,), (1,)), ((), ())), preferred_element_type=F32
                    )
                part[lax.rem(k, ring), o] = total
                return 0

            lax.fori_loop(0, nz, rows_of, 0)

        up_k = k - z

        @when(valid(up_k) & (z < nz - 1))
        def _():
            for o in range(nz - 1, 0, -1):
                @when(o > z)
                def _():
                    @when(z > 0)
                    def _():
                        d_copy(True, o, up_k).wait_recv()
                        sbuf[o, up_k] = (part[lax.rem(up_k, ring), o] + rbuf[o + 1, up_k].astype(F32)).astype(BF16)

                    @when(z == 0)
                    def _():
                        sbuf[o, up_k] = part[lax.rem(up_k, ring), o].astype(BF16)

                    d_copy(True, o, up_k).start()

        down_k = k - (nz - 1 - z)

        @when(valid(down_k) & (z > 0))
        def _():
            for o in range(nz - 1):
                @when(o < z)
                def _():
                    @when(z < nz - 1)
                    def _():
                        d_copy(False, o, down_k).wait_recv()
                        sbuf[o, down_k] = (part[lax.rem(down_k, ring), o] + rbuf[o, down_k].astype(F32)).astype(BF16)

                    @when(z == nz - 1)
                    def _():
                        sbuf[o, down_k] = part[lax.rem(down_k, ring), o].astype(BF16)

                    d_copy(False, o, down_k).start()

        own_k = k - lag

        @when(valid(own_k))
        def _():
            acc[...] = part[lax.rem(own_k, ring), z]

            @when(z > 0)
            def _():
                d_copy(True, z, own_k).wait_recv()
                acc[...] += rbuf[z + 1, own_k].astype(F32)

            @when(z < nz - 1)
            def _():
                d_copy(False, z, own_k).wait_recv()
                acc[...] += rbuf[z, own_k].astype(F32)

            adjoint_state(own_k)

        far_k = k - nz

        @when(valid(far_k))
        def _():
            adjoint_filter(far_k)

        h = s - nk + 1

        @when((h >= 0) & (h < nz))
        def _():
            blocks(0, h)

        pair = (k - nk) * 2

        @when((pair >= 0) & (pair < nz))
        def _():
            def both(i, _):
                for src in range(1, nx):
                    blocks(src, pair + i)
                return 0

            lax.fori_loop(0, 2, both, 0)

        @when(s == nk + 1 + distance)
        def _():
            finish(0)

        @when(k == nk + 2 + lax.div(distance, 2))
        def _():
            for src in range(1, nx):
                finish(src)

        return 0

    lax.fori_loop(AHEAD, AHEAD + nk + nz, step, 0)

    @when(stays)
    def _():
        yout[...] = yfs[...]

    @when(leaves)
    def _():
        def land(q, _):
            y_copy(q).wait()
            return 0

        lax.fori_loop(0, nk, land, 0)
        yout[...] = yfr[...]

    @when(leaves & on_line)
    def _():
        for h in range(halves):
            cot_copy(h).wait_send()

    @when(jnp.logical_not(on_line))
    def _():
        for h in range(halves):
            side_copy(h).wait_send()

    @when(side_leaves)
    def _():
        for h in range(halves):
            side_relay(h).wait_send()

    for h in range(halves):
        for d in range(ny):
            spread(d, h).wait_send()
        for d in range(1, ny):
            relay(d, h).wait_send()

    def drain(k, _):
        for d in range(1, nx):
            w_copy(d, k).wait_send()
        for slot in range(ny):
            a_copy((1 - c) * ny + slot, k).wait_send()
        for d in range(1, ny):
            b_copy(lax.rem(y + d, ny), k).wait_send()
        for o in range(nz):
            @when((z < nz - 1) & (o <= z))
            def _():
                x_copy(True, o, k).wait_send()

            @when((z > 0) & (o >= z))
            def _():
                x_copy(False, o, k).wait_send()

            @when(o > z)
            def _():
                d_copy(True, o, k).wait_send()

            @when(o < z)
            def _():
                d_copy(False, o, k).wait_send()

        for hop in range(1, hops + 1):
            @when(index + hop < ctx)
            def _():
                f_copy(hop, k).wait_send()

            @when(index - hop >= 0)
            def _():
                s_copy(hop, k).wait_send()

        return 0

    lax.fori_loop(0, nk, drain, 0)


def fused_call(sizes, tokens, cot, weight, parameters):
    nz, nx, ny, hops, modes = sizes
    length, channels = cot.shape
    width = weight.shape[1]
    nk = channels // COLS
    vmem = pl.BlockSpec(memory_space=pltpu.VMEM)
    hbm = pl.BlockSpec(memory_space=pl.ANY)
    token = jax.ShapeDtypeStruct((length, channels), BF16)
    dma = pltpu.SemaphoreType.DMA
    near = max(ny - 1, 1)
    wide_x = max(nx - 1, 1)
    flops = 8 * nz * length * channels * width * nx // 2
    return pl.pallas_call(
        functools.partial(fused, sizes),
        out_shape=(token,) * 4,
        in_specs=[vmem] * 3 + [hbm] * 2 + [vmem] * len(parameters),
        out_specs=(vmem,) * 4,
        scratch_shapes=[
            pltpu.VMEM((channels, width), BF16),
            pltpu.VMEM((wide_x, channels, width), BF16),
            pltpu.VMEM((nz, length, channels), BF16),
            pltpu.VMEM((nz, nz, length, COLS), F32),
            pltpu.VMEM((nz, nk, length, COLS), BF16),
            pltpu.VMEM((nz + 1, nk, length, COLS), BF16),
            pltpu.VMEM((nz, length, channels), BF16),
            pltpu.VMEM((ny, length, channels), BF16),
            pltpu.VMEM((ny, length, channels), BF16),
            pltpu.VMEM((near, length, channels), BF16),
            pltpu.VMEM((near, length, channels), BF16),
            pltpu.VMEM((length, channels), F32),
            pltpu.VMEM((length, channels), F32),
            pltpu.VMEM((length, channels), BF16),
            pltpu.VMEM((length, channels), BF16),
            pltpu.VMEM((length, COLS), F32),
            pltpu.VMEM((length, channels), F32),
            pltpu.VMEM((length, channels), BF16),
            pltpu.VMEM((nk, modes, COLS), F32),
            pltpu.VMEM((hops, nk, modes, COLS), F32),
            pltpu.VMEM((nk, modes, COLS), F32),
            pltpu.VMEM((hops, nk, modes, COLS), F32),
            pltpu.VMEM((length, channels), BF16),
            dma((2,)),
            dma((PIECES,)), dma((PIECES,)),
            dma((wide_x, nk)), dma((wide_x, nk)),
            dma((PIECES,)), dma((PIECES,)),
            dma((ny, PIECES)), dma((ny, PIECES)),
            dma((near, PIECES)), dma((near, PIECES)),
            dma((2, nz, nk)), dma((nz, nk)),
            dma((nz, nk)), dma((nz + 1, nk)),
            dma((ny, nk)), dma((ny, nk)),
            dma((near, nk)), dma((near, nk)),
            dma((nk,)), dma((nk,)),
            dma((hops, nk)), dma((hops, nk)),
            dma((hops, nk)), dma((hops, nk)),
        ],
        compiler_params=pltpu.CompilerParams(
            collective_id=0, has_side_effects=True, vmem_limit_bytes=63 * 2**20
        ),
        cost_estimate=pl.CostEstimate(flops=flops, bytes_accessed=16 * 2**20, transcendentals=0),
    )(*tokens, cot, weight, *parameters)


def on_device(
    query_branch,
    key_branch,
    value_branch,
    out_cotangent,
    out_weight,
    residues,
    decay_rates,
    skip_gains,
    record_lengths,
):
    length, channels = query_branch.shape
    modes = residues.shape[1]
    nz, nx, ny = lax.axis_size("z"), lax.axis_size("x"), lax.axis_size("y")
    ctx = nz * nx
    hops = -(-(length * ctx // 4) // length)
    index = lax.axis_index("z") * nx + lax.axis_index("x")

    records = record_lengths.shape[0]
    before = jnp.arange(records)[:, None] > jnp.arange(records)[None, :]
    offsets = jnp.sum(jnp.where(before, record_lengths[None, :], 0), axis=1)
    blocks = jnp.arange(ctx, dtype=jnp.int32) * length
    closed = jnp.any(
        (offsets[None, :] >= blocks[:, None]) & (offsets[None, :] < blocks[:, None] + length), axis=1
    ).astype(jnp.int32)
    at = jnp.arange(length, dtype=jnp.int32)
    local = offsets - index * length

    def segment_of(pos):
        shape = (1,) * pos.ndim
        starts = local.reshape((-1,) + shape)
        return jnp.sum(((starts >= 0) & (starts <= pos[None])).astype(jnp.int32), axis=0)

    segment = segment_of(at)
    final = jnp.sum(((local >= 0) & (local < length)).astype(jnp.int32))
    first = (segment == 0).astype(F32)[None, :]
    last = (segment == final).astype(F32)[None, :]
    mask = ((at[:, None] >= at[None, :]) & (segment[:, None] == segment[None, :])).astype(F32)

    coeffs = residues * jnp.sqrt(1.0 - jnp.exp(-2.0 * decay_rates))
    rates_rows = jnp.broadcast_to(decay_rates.reshape(-1, 1), (decay_rates.size, LANES))
    coeff_rows = jnp.broadcast_to(coeffs.reshape(-1, 1), (coeffs.size, LANES))
    through = jnp.repeat(jnp.exp(-decay_rates * length).T, GSIZE, axis=1)
    skip = skip_gains[None, :]
    def opened(direction):
        passed = jnp.clip(index - direction * (1 + jnp.arange(hops)), 0, ctx - 1)
        return jnp.broadcast_to((1.0 - closed[passed].astype(F32))[:, None], (hops, LANES))

    doors = jnp.concatenate([opened(1), opened(-1)], axis=0)
    return fused_call(
        (nz, nx, ny, hops, modes),
        (query_branch, key_branch, value_branch), out_cotangent, out_weight,
        (rates_rows, coeff_rows, skip, through, doors, first, last, mask, mask.T),
    )


def solution(mesh):
    ctx, tp = mesh.devices.shape
    fine = Mesh(mesh.devices.reshape(tp, ctx // tp, tp // CORES, CORES), ("z", "x", "y", "c"))
    tokens = P(("z", "x"), ("y", "c"))
    placed = (
        tokens,
        tokens,
        tokens,
        tokens,
        P(("y", "c"), ("z", "x")),
        P(("y", "c"), None),
        P(("y", "c"), None),
        P(("y", "c")),
        P(),
    )
    return jax.shard_map(
        on_device,
        mesh=fine,
        in_specs=placed,
        out_specs=(tokens, tokens, tokens, tokens),
        check_vma=False,
    )
```

```python
import functools

import jax
import jax.numpy as jnp
from jax import lax
from jax.experimental import pallas as pl
from jax.experimental.pallas import tpu as pltpu
from jax.sharding import Mesh, PartitionSpec as P

GSIZE = 16
LANES = 128
TILE_GROUPS = LANES // GSIZE
CORES = 2
COLS = 256
PIECES = 4
AHEAD = 2
F32, BF16 = jnp.float32, jnp.bfloat16
MESH = pl.DeviceIdType.MESH


def split(a):
    hi = a.astype(BF16)
    return hi, (a - hi.astype(F32)).astype(BF16)


def positions(rows, length):
    return lax.broadcasted_iota(jnp.int32, (rows, length), 1).astype(F32)


def inflow_rows(rates, coeffs, pos, first):
    return coeffs * jnp.exp(-rates * (pos + 1.0)) * first


def outflow_rows(rates, pos, last):
    return jnp.exp(-rates * (pos.shape[1] - 1.0 - pos)) * last


def own_lanes(shape, group):
    lane = lax.broadcasted_iota(jnp.int32, shape, 1)
    return (lane >= group * GSIZE) & (lane < (group + 1) * GSIZE)


def weighted_state(rows, x, modes):
    hi, lo = split(rows)
    full = jnp.dot(hi, x, preferred_element_type=F32) + jnp.dot(lo, x, preferred_element_type=F32)
    state = jnp.zeros((modes, LANES), F32)
    for g in range(TILE_GROUPS):
        part = full[g * modes : (g + 1) * modes]
        state = jnp.where(own_lanes(part.shape, g), part, state)
    return state


def contract_first(a, b):
    return lax.dot_general(a, b, (((0,), (0,)), ((), ())), preferred_element_type=F32)


def from_state(rows, state, modes):
    blocks = [jnp.where(own_lanes(state.shape, g), state, 0.0) for g in range(TILE_GROUPS)]
    state_rows = jnp.concatenate(blocks, axis=0)
    r_hi, r_lo = split(rows)
    s_hi, s_lo = split(state_rows)
    return contract_first(r_hi, s_hi) + contract_first(r_lo, s_hi) + contract_first(r_hi, s_lo)


def convolve(left, right, mask, x, modes):
    l_hi, l_lo = split(left)
    r_hi, r_lo = split(right)
    total = jnp.zeros(x.shape, F32)
    for g in range(TILE_GROUPS):
        rows = slice(g * modes, (g + 1) * modes)
        a = jnp.concatenate([l_hi[rows], l_lo[rows], l_hi[rows]], axis=0)
        b = jnp.concatenate([r_hi[rows], r_hi[rows], r_lo[rows]], axis=0)
        kernel = (contract_first(a, b) * mask).astype(BF16)
        own = jnp.where(own_lanes(x.shape, g), x, jnp.zeros_like(x))
        total = total + jnp.dot(kernel, own, preferred_element_type=F32)
    return total


def when(cond):
    return pl.when(cond)


def fused(sizes, lengths, query, key, value, cot, w_hbm, rates_in, coeffs_in, skip,
          yout, qgrad, kgrad, vgrad,
          w, wg, dyg, part, sbuf, rbuf, xg, yas, yar, ybs, ybr, yp, yf, yfs, yfr, acc, mixed, fgrad, fown, fin, bown, bin_, crelay,
          rates, coeffs, first, last, mask, mask_t,
          lsem, rss, rrs, wss, wrs, css, crs, gss, grs, fss, frs, xss, xrs, dss, drs, ass, ars, bss, brs, yss, yrs,
          sfs, sfr, sbs, sbr):
    nz, nx, ny, hops, modes = sizes
    length, channels = query.shape
    width = w.shape[1]
    ctx = nz * nx
    rows = TILE_GROUPS * modes
    ring = part.shape[0]
    tiles = COLS // LANES
    nk = channels // COLS
    nw = width // COLS
    halves = PIECES
    hrows = length // halves
    z, x = lax.axis_index("z"), lax.axis_index("x")
    y, c = lax.axis_index("y"), lax.axis_index("c")
    t = y * CORES + c
    mine = c * ny + lax.rem(y - z + nz * ny, ny)
    holder = (t, x, lax.rem(z + t, ny), lax.div(z, ny))
    owner = (mine, x, lax.div(z, CORES), lax.rem(z, CORES))
    stays = (t == z) & (y == lax.rem(z + t, ny)) & (c == lax.div(z, ny))
    leaves = jnp.logical_not(stays)
    two_lines = ny == 2
    on_line = y == lax.rem(z + c, ny)
    via = (z, x, lax.rem(y + 1, ny), c)
    side_t = lax.rem(y + 1, ny) * CORES + c
    side_holder = (side_t, x, y, lax.div(z, ny))
    side_stays = on_line & (side_t == z) & (c == lax.div(z, ny))
    side_leaves = on_line & jnp.logical_not(side_stays)
    side_source = (mine, x, y, lax.rem(z, CORES))
    by_side = (y != lax.div(z, CORES)) & jnp.logical_not((mine == z) & (c == lax.rem(z, CORES)))
    if not two_lines:
        on_line = y == y
        side_stays = side_leaves = by_side = y != y
    arrives = leaves & jnp.logical_not(side_stays)
    twin = (z, x, y, 1 - c)
    index = z * nx + x

    def along(move):
        return (lax.div(index + move, nx), lax.rem(index + move, nx), y, c)

    def cp(src, dst, ssem, rsem, dev):
        return pltpu.make_async_remote_copy(
            src_ref=src, dst_ref=dst, send_sem=ssem, recv_sem=rsem, device_id=dev, device_id_type=MESH
        )

    def cols(i):
        return pl.ds(pl.multiple_of(i * COLS, COLS), COLS)

    barrier = pltpu.get_barrier_semaphore()
    for dx in range(1, nx):
        pl.semaphore_signal(barrier, 1, device_id=(z, lax.rem(x + dx, nx), y, c), device_id_type=MESH)
    for dy in range(1, ny):
        pl.semaphore_signal(barrier, 1, device_id=(z, x, lax.rem(y + dy, ny), c), device_id_type=MESH)
    pl.semaphore_signal(barrier, 1, device_id=twin, device_id_type=MESH)

    @when(z > 0)
    def _():
        pl.semaphore_signal(barrier, 1, device_id=(z - 1, x, y, c), device_id_type=MESH)

    @when(z < nz - 1)
    def _():
        pl.semaphore_signal(barrier, 1, device_id=(z + 1, x, y, c), device_id_type=MESH)

    @when(leaves)
    def _():
        pl.semaphore_signal(barrier, 1, device_id=holder, device_id_type=MESH)
        pl.semaphore_signal(barrier, 1, device_id=owner, device_id_type=MESH)

    @when(side_leaves)
    def _():
        pl.semaphore_signal(barrier, 1, device_id=side_holder, device_id_type=MESH)

    @when(by_side)
    def _():
        pl.semaphore_signal(barrier, 1, device_id=side_source, device_id_type=MESH)

    def one(cond):
        return cond.astype(jnp.int32)

    greetings = (nx - 1) + (ny - 1) + 1 + one(z > 0) + one(z < nz - 1) + 2 * one(leaves) + one(side_leaves) + one(by_side)
    for hop in range(1, hops + 1):
        for move in (hop, -hop):
            there = (index + move >= 0) & (index + move < ctx)
            greetings = greetings + one(there)

            @when(there)
            def _():
                pl.semaphore_signal(barrier, 1, device_id=along(move), device_id_type=MESH)

    base = index * length
    row_pos = lax.broadcasted_iota(jnp.int32, (1, length), 1)
    col_pos = lax.broadcasted_iota(jnp.int32, (length, 1), 0)
    row_segment, col_segment = jnp.zeros_like(row_pos), jnp.zeros_like(col_pos)
    offset, started = jnp.int32(0), jnp.int32(0)
    passed = [[index - way * hop for hop in range(1, hops + 1)] for way in (1, -1)]
    starts_in = [[jnp.int32(0)] * hops for _ in range(2)]

    def starts(block):
        return one((offset >= block * length) & (offset < block * length + length))

    for record in range(lengths.shape[0]):
        here = jnp.where(offset >= base, offset - base, length)
        row_segment += (row_pos >= here).astype(jnp.int32)
        col_segment += (col_pos >= here).astype(jnp.int32)
        started += starts(index)
        for way in range(2):
            starts_in[way] = [starts_in[way][i] + starts(passed[way][i]) for i in range(hops)]
        offset += lengths[record]

    opened = [[jnp.where(count > 0, 0.0, 1.0) for count in counts] for counts in starts_in]
    first[...] = (row_segment == 0).astype(F32)
    last[...] = (row_segment == started).astype(F32)
    together = col_segment == row_segment
    mask[...] = (together & (col_pos >= row_pos)).astype(F32)
    mask_t[...] = (together & (col_pos <= row_pos)).astype(F32)

    def spread_out(i, _):
        groups = pl.ds(pl.multiple_of(i * TILE_GROUPS, TILE_GROUPS), TILE_GROUPS)
        at = pl.ds(pl.multiple_of(i * rows, rows), rows)
        lane = lax.broadcasted_iota(jnp.int32, (TILE_GROUPS, modes, modes), 2)
        mode = lax.broadcasted_iota(jnp.int32, (TILE_GROUPS, modes, modes), 1)
        for source, target in ((rates_in, rates), (coeffs_in, coeffs)):
            table = jnp.broadcast_to(source[groups, :][:, None, :], (TILE_GROUPS, modes, modes))
            picked = jnp.where(lane == mode, table, 0.0).reshape(rows, modes)
            target[at, :] = jnp.broadcast_to(jnp.sum(picked, axis=1, keepdims=True), (rows, LANES))
        return 0

    lax.fori_loop(0, channels // LANES, spread_out, 0)
    pl.semaphore_wait(barrier, greetings)

    def w_copy(d, k):
        return cp(w_hbm.at[cols(k)], wg.at[d - 1, cols(k)], wss.at[d - 1, k], wrs.at[d - 1, k], (z, lax.rem(x + d, nx), y, c))

    def half(h):
        return pl.ds(h * hrows, hrows)

    def cot_copy(h):
        return cp(cot.at[half(h)], dyg.at[z, half(h)], css.at[h], crs.at[h], holder)

    def side_copy(h):
        return cp(cot.at[half(h)], crelay.at[half(h)], rss.at[h], rrs.at[h], via)

    def side_relay(h):
        return cp(crelay.at[half(h)], dyg.at[z, half(h)], rss.at[h], crs.at[h], side_holder)

    def cot_arrival(h):
        return cp(cot.at[half(h)], dyg.at[mine, half(h)], css.at[h], crs.at[h], holder)

    def held_by(core, d):
        return core * ny + lax.rem(y - d - z + nz * ny + ny, ny)

    def spread(d, h):
        dev = twin if d == 0 else (z, x, lax.rem(y + d, ny), c)
        return cp(dyg.at[mine, half(h)], dyg.at[mine, half(h)], gss.at[d, h], grs.at[d, h], dev)

    def spread_arrival(d, h):
        slot = held_by(1 - c if d == 0 else c, d)
        return cp(dyg.at[slot, half(h)], dyg.at[slot, half(h)], gss.at[d, h], grs.at[d, h], twin)

    def relay(d, h):
        slot = held_by(c, d)
        return cp(dyg.at[slot, half(h)], dyg.at[slot, half(h)], fss.at[d - 1, h], frs.at[d - 1, h], twin)

    def relay_arrival(d, h):
        slot = held_by(1 - c, d)
        return cp(dyg.at[slot, half(h)], dyg.at[slot, half(h)], fss.at[d - 1, h], frs.at[d - 1, h], twin)

    def x_copy(up, o, j):
        dev = (z + 1, x, y, c) if up else (z - 1, x, y, c)
        side = 0 if up else 1
        return cp(xg.at[o, :, cols(j)], xg.at[o, :, cols(j)], xss.at[side, o, j], xrs.at[o, j], dev)

    def d_copy(up, o, k):
        dev = (z + 1, x, y, c) if up else (z - 1, x, y, c)
        slot = o + 1 if up else o
        return cp(sbuf.at[o, k], rbuf.at[slot, k], dss.at[o, k], drs.at[slot, k], dev)

    def a_copy(o, q):
        slot = lax.rem(o, ny)
        return cp(yas.at[slot, :, cols(q)], yar.at[slot, :, cols(q)], ass.at[slot, q], ars.at[slot, q], twin)

    def b_copy(yd, q):
        slot = lax.rem(yd + ny - y, ny) - 1
        return cp(ybs.at[slot, :, cols(q)], ybr.at[slot, :, cols(q)], bss.at[slot, q], brs.at[slot, q], (z, x, yd, c))

    def y_copy(q):
        return cp(yfs.at[:, cols(q)], yfr.at[:, cols(q)], yss.at[q], yrs.at[q], owner)

    def f_copy(hop, j):
        return cp(fown.at[j], fin.at[hop - 1, j], sfs.at[hop - 1, j], sfr.at[hop - 1, j], along(hop))

    def s_copy(hop, j):
        return cp(bown.at[j], bin_.at[hop - 1, j], sbs.at[hop - 1, j], sbr.at[hop - 1, j], along(-hop))

    pos = positions(rows, length)

    def lanes(j, i):
        return pl.ds(pl.multiple_of(j * COLS + i * LANES, LANES), LANES)

    def parameters(ref, j, i):
        tile = ref[pl.ds(pl.multiple_of((j * tiles + i) * rows, rows), rows), :]
        return jnp.concatenate([tile] * (length // LANES), axis=1)

    def mode_rates(j, i):
        tile = rates[pl.ds(pl.multiple_of((j * tiles + i) * rows, rows), rows), :]
        result = tile[:modes]
        for g in range(1, TILE_GROUPS):
            result = jnp.where(own_lanes(result.shape, g), tile[g * modes : (g + 1) * modes], result)
        return result

    def gated_of(at):
        return (key[:, at].astype(F32) * value[:, at].astype(F32)).astype(BF16)

    def forward_state(j):
        for i in range(tiles):
            r = parameters(rates, j, i)
            fown[j, :, i * LANES : (i + 1) * LANES] = weighted_state(
                outflow_rows(r, pos, last[...]), gated_of(lanes(j, i)), modes
            )
        for hop in range(1, hops + 1):
            @when(index + hop < ctx)
            def _():
                f_copy(hop, j).start()

    def entering(j, copy, ref, sign, way):
        acc[:modes, :] = jnp.zeros((modes, COLS), F32)
        factor = jnp.ones((modes, COLS), F32)
        through = jnp.exp(-length * jnp.concatenate([mode_rates(j, i) for i in range(tiles)], axis=1))
        for hop in range(1, hops + 1):
            there = (index - hop >= 0) if sign > 0 else (index + hop < ctx)
            now = factor

            @when(there)
            def _():
                copy(hop, j).wait_recv()
                acc[:modes, :] += now * ref[hop - 1, j]

            if hop < hops:
                factor = factor * through * opened[way][hop - 1]

    def forward_filter(j):
        entering(j, f_copy, fin, 1, 0)
        for i in range(tiles):
            at = lanes(j, i)
            r, co = parameters(rates, j, i), parameters(coeffs, j, i)
            g = gated_of(at)
            half = length / 2.0
            total = convolve(co * jnp.exp(-r * (pos - half)), jnp.exp(r * (pos - half)), mask[...], g, modes)
            total = total + from_state(
                inflow_rows(r, co, pos, first[...]), acc[:modes, i * LANES : (i + 1) * LANES], modes
            )
            result = total.astype(BF16).astype(F32) + skip[:, at] * g.astype(F32)
            mixed[:, at] = result
            xg[z, :, at] = (query[:, at].astype(F32) * result).astype(BF16)

        @when(z < nz - 1)
        def _():
            x_copy(True, z, j).start()

        @when(z > 0)
        def _():
            x_copy(False, z, j).start()

    def adjoint_state(j):
        for i in range(tiles):
            at = lanes(j, i)
            r, co = parameters(rates, j, i), parameters(coeffs, j, i)
            g = acc[:, i * LANES : (i + 1) * LANES].astype(BF16).astype(F32)
            f = (g * query[:, at].astype(F32)).astype(BF16)
            fgrad[:, at] = f
            qgrad[:, at] = (g * mixed[:, at]).astype(BF16)
            bown[j, :, i * LANES : (i + 1) * LANES] = weighted_state(inflow_rows(r, co, pos, first[...]), f, modes)
        for hop in range(1, hops + 1):
            @when(index - hop >= 0)
            def _():
                s_copy(hop, j).start()

    def adjoint_filter(j):
        entering(j, s_copy, bin_, -1, 1)
        for i in range(tiles):
            at = lanes(j, i)
            r, co = parameters(rates, j, i), parameters(coeffs, j, i)
            f = fgrad[:, at]
            half = length / 2.0
            total = convolve(jnp.exp(r * (pos - half)), co * jnp.exp(-r * (pos - half)), mask_t[...], f, modes)
            total = total + from_state(
                outflow_rows(r, pos, last[...]), acc[:modes, i * LANES : (i + 1) * LANES], modes
            )
            result = total.astype(BF16).astype(F32) + skip[:, at] * f.astype(F32)
            kgrad[:, at] = (result * value[:, at].astype(F32)).astype(BF16)
            vgrad[:, at] = (result * key[:, at].astype(F32)).astype(BF16)

    own_cot = pltpu.make_async_copy(cot, dyg.at[z], lsem.at[1])
    own_w = pltpu.make_async_copy(w_hbm, w, lsem.at[0])

    def start_w(k):
        for d in range(1, nx):
            w_copy(d, k).start()

    def repeat(lo, hi, body):
        def run(j, _):
            body(j)
            return 0

        lax.fori_loop(lo, hi, run, 0)

    def valid(k):
        return (k >= 0) & (k < nk)

    def pass_on(s):
        for h in range(1, nz):
            j = s - (h - 1)
            for up in (True, False):
                o = z - h if up else z + h
                there = (o >= 0) if up else (o < nz)
                further = (z < nz - 1) if up else (z > 0)

                @when(valid(j) & there)
                def _():
                    x_copy(up, o, j).wait_recv()

                    @when(further)
                    def _():
                        x_copy(up, o, j).start()

    repeat(0, nk, forward_state)

    @when(leaves & on_line)
    def _():
        for h in range(halves):
            cot_copy(h).start()

    @when(jnp.logical_not(on_line))
    def _():
        for h in range(halves):
            side_copy(h).start()

    @when(stays)
    def _():
        own_cot.start()

    repeat(0, nk, start_w)
    own_w.start()
    repeat(0, nk // 2, forward_filter)

    if two_lines:
        @when(on_line)
        def _():
            for h in range(halves):
                side_copy(h).wait_recv()

                @when(side_leaves)
                def _():
                    side_relay(h).start()

                @when(side_stays)
                def _():
                    dyg[z, half(h)] = crelay[half(h)]

    repeat(nk // 2, nk, forward_filter)
    repeat(0, AHEAD // 2, pass_on)

    @when(stays)
    def _():
        own_cot.wait()

    for h in range(halves):
        @when(arrives)
        def _():
            cot_arrival(h).wait_recv()

        for d in range(ny):
            spread(d, h).start()

    repeat(AHEAD // 2, AHEAD, pass_on)

    for h in range(halves):
        for d in range(1, ny):
            spread_arrival(d, h).wait_recv()
            relay(d, h).start()
    own_w.wait()
    for h in range(halves):
        spread_arrival(0, h).wait_recv()
        for d in range(1, ny):
            relay_arrival(d, h).wait_recv()

    lag = jnp.maximum(z, nz - 1 - z)

    def column_of(src, i):
        return lax.rem(x + nx - src, nx) * nw + i

    def block(src, o):
        slot, core = lax.rem(o, ny), lax.div(o, ny)
        yd = lax.rem(o + z, ny)

        def column(i, _):
            q = column_of(src, i)
            ref = w if src == 0 else wg.at[src - 1]
            p = jnp.dot(xg[o], ref[:, cols(i)], preferred_element_type=F32)

            @when(c != core)
            def _():
                yas[slot, :, cols(q)] = p.astype(BF16)
                a_copy(o, q).start()

            @when(c == core)
            def _():
                yp[:, cols(q)] = p

            return 0

        lax.fori_loop(0, nw, column, 0)

        @when(c == core)
        def _():
            def add(i, _):
                q = column_of(src, i)
                a_copy(o, q).wait_recv()
                total = yp[:, cols(q)] + yar[slot, :, cols(q)].astype(F32)

                @when(yd != y)
                def _():
                    ybs[lax.rem(yd + ny - y, ny) - 1, :, cols(q)] = total.astype(BF16)
                    b_copy(yd, q).start()

                @when(yd == y)
                def _():
                    yf[:, cols(q)] = total

                return 0

            lax.fori_loop(0, nw, add, 0)

    def blocks(src, h):
        def side(i, _):
            o = z + h * (1 - 2 * i)

            @when((o >= 0) & (o < nz) & ((h > 0) | (i == 0)))
            def _():
                block(src, o)

            return 0

        lax.fori_loop(0, 2, side, 0)

    def finish(src):
        def last_sum(i, _):
            q = column_of(src, i)
            total = yf[:, cols(q)]
            for d in range(1, ny):
                cp(ybs.at[d - 1, :, cols(q)], ybr.at[d - 1, :, cols(q)], bss.at[d - 1, q], brs.at[d - 1, q], twin).wait_recv()
                total = total + ybr[d - 1, :, cols(q)].astype(F32)

            yfs[:, cols(q)] = total.astype(BF16)

            @when(leaves)
            def _():
                y_copy(q).start()

            return 0

        lax.fori_loop(0, nw, last_sum, 0)

    distance = jnp.maximum(mine - z, z - mine)

    def step(s, _):
        k = s - AHEAD

        @when(k < nk)
        def _():
            for d in range(1, nx):
                w_copy(d, k).wait_recv()
            own_cols = pl.ds(pl.multiple_of(x * width, LANES), width)

            def rows_of(o, _):
                total = lax.dot_general(
                    dyg[o, :, own_cols], w[cols(k), :], (((1,), (1,)), ((), ())), preferred_element_type=F32
                )
                for d in range(1, nx):
                    from_cols = pl.ds(pl.multiple_of(lax.rem(x + nx - d, nx) * width, LANES), width)
                    total = total + lax.dot_general(
                        dyg[o, :, from_cols], wg[d - 1, cols(k), :], (((1,), (1,)), ((), ())), preferred_element_type=F32
                    )
                part[lax.rem(k, ring), o] = total
                return 0

            lax.fori_loop(0, nz, rows_of, 0)

        up_k = k - z

        @when(valid(up_k) & (z < nz - 1))
        def _():
            for o in range(nz - 1, 0, -1):
                @when(o > z)
                def _():
                    @when(z > 0)
                    def _():
                        d_copy(True, o, up_k).wait_recv()
                        sbuf[o, up_k] = (part[lax.rem(up_k, ring), o] + rbuf[o + 1, up_k].astype(F32)).astype(BF16)

                    @when(z == 0)
                    def _():
                        sbuf[o, up_k] = part[lax.rem(up_k, ring), o].astype(BF16)

                    d_copy(True, o, up_k).start()

        down_k = k - (nz - 1 - z)

        @when(valid(down_k) & (z > 0))
        def _():
            for o in range(nz - 1):
                @when(o < z)
                def _():
                    @when(z < nz - 1)
                    def _():
                        d_copy(False, o, down_k).wait_recv()
                        sbuf[o, down_k] = (part[lax.rem(down_k, ring), o] + rbuf[o, down_k].astype(F32)).astype(BF16)

                    @when(z == nz - 1)
                    def _():
                        sbuf[o, down_k] = part[lax.rem(down_k, ring), o].astype(BF16)

                    d_copy(False, o, down_k).start()

        pass_on(s)

        own_k = k - lag

        @when(valid(own_k))
        def _():
            acc[...] = part[lax.rem(own_k, ring), z]

            @when(z > 0)
            def _():
                d_copy(True, z, own_k).wait_recv()
                acc[...] += rbuf[z + 1, own_k].astype(F32)

            @when(z < nz - 1)
            def _():
                d_copy(False, z, own_k).wait_recv()
                acc[...] += rbuf[z, own_k].astype(F32)

            adjoint_state(own_k)

        far_k = k - nz

        @when(valid(far_k))
        def _():
            adjoint_filter(far_k)

        h = s - nk + 1

        @when((h >= 0) & (h < nz))
        def _():
            blocks(0, h)

        pair = (k - nk) * 2

        @when((pair >= 0) & (pair < nz))
        def _():
            def both(i, _):
                for src in range(1, nx):
                    blocks(src, pair + i)
                return 0

            lax.fori_loop(0, 2, both, 0)

        @when(s == nk + 1 + distance)
        def _():
            finish(0)

        @when(k == nk + 2 + lax.div(distance, 2))
        def _():
            for src in range(1, nx):
                finish(src)

        return 0

    lax.fori_loop(AHEAD, AHEAD + nk + nz, step, 0)

    @when(stays)
    def _():
        yout[...] = yfs[...]

    @when(leaves)
    def _():
        def land(q, _):
            y_copy(q).wait()
            return 0

        lax.fori_loop(0, nk, land, 0)
        yout[...] = yfr[...]

    @when(leaves & on_line)
    def _():
        for h in range(halves):
            cot_copy(h).wait_send()

    @when(jnp.logical_not(on_line))
    def _():
        for h in range(halves):
            side_copy(h).wait_send()

    @when(side_leaves)
    def _():
        for h in range(halves):
            side_relay(h).wait_send()

    for h in range(halves):
        for d in range(ny):
            spread(d, h).wait_send()
        for d in range(1, ny):
            relay(d, h).wait_send()

    def drain(k, _):
        for d in range(1, nx):
            w_copy(d, k).wait_send()
        for slot in range(ny):
            a_copy((1 - c) * ny + slot, k).wait_send()
        for d in range(1, ny):
            b_copy(lax.rem(y + d, ny), k).wait_send()
        for o in range(nz):
            @when((z < nz - 1) & (o <= z))
            def _():
                x_copy(True, o, k).wait_send()

            @when((z > 0) & (o >= z))
            def _():
                x_copy(False, o, k).wait_send()

            @when(o > z)
            def _():
                d_copy(True, o, k).wait_send()

            @when(o < z)
            def _():
                d_copy(False, o, k).wait_send()

        for hop in range(1, hops + 1):
            @when(index + hop < ctx)
            def _():
                f_copy(hop, k).wait_send()

            @when(index - hop >= 0)
            def _():
                s_copy(hop, k).wait_send()

        return 0

    lax.fori_loop(0, nk, drain, 0)


def fused_call(sizes, lengths, tokens, cot, weight, parameters):
    nz, nx, ny, hops, modes = sizes
    length, channels = cot.shape
    width = weight.shape[1]
    nk = channels // COLS
    vmem = pl.BlockSpec(memory_space=pltpu.VMEM)
    hbm = pl.BlockSpec(memory_space=pl.ANY)
    token = jax.ShapeDtypeStruct((length, channels), BF16)
    dma = pltpu.SemaphoreType.DMA
    near = max(ny - 1, 1)
    wide_x = max(nx - 1, 1)
    flops = 8 * nz * length * channels * width * nx // 2
    return pl.pallas_call(
        functools.partial(fused, sizes),
        out_shape=(token,) * 4,
        in_specs=[pl.BlockSpec(memory_space=pltpu.SMEM)] + [vmem] * 3 + [hbm] * 2 + [vmem] * len(parameters),
        out_specs=(vmem,) * 4,
        scratch_shapes=[
            pltpu.VMEM((channels, width), BF16),
            pltpu.VMEM((wide_x, channels, width), BF16),
            pltpu.VMEM((nz, length, channels), BF16),
            pltpu.VMEM((nz, nz, length, COLS), F32),
            pltpu.VMEM((nz, nk, length, COLS), BF16),
            pltpu.VMEM((nz + 1, nk, length, COLS), BF16),
            pltpu.VMEM((nz, length, channels), BF16),
            pltpu.VMEM((ny, length, channels), BF16),
            pltpu.VMEM((ny, length, channels), BF16),
            pltpu.VMEM((near, length, channels), BF16),
            pltpu.VMEM((near, length, channels), BF16),
            pltpu.VMEM((length, channels), F32),
            pltpu.VMEM((length, channels), F32),
            pltpu.VMEM((length, channels), BF16),
            pltpu.VMEM((length, channels), BF16),
            pltpu.VMEM((length, COLS), F32),
            pltpu.VMEM((length, channels), F32),
            pltpu.VMEM((length, channels), BF16),
            pltpu.VMEM((nk, modes, COLS), F32),
            pltpu.VMEM((hops, nk, modes, COLS), F32),
            pltpu.VMEM((nk, modes, COLS), F32),
            pltpu.VMEM((hops, nk, modes, COLS), F32),
            pltpu.VMEM((length, channels), BF16),
            pltpu.VMEM((channels // GSIZE * modes, LANES), F32),
            pltpu.VMEM((channels // GSIZE * modes, LANES), F32),
            pltpu.VMEM((1, length), F32),
            pltpu.VMEM((1, length), F32),
            pltpu.VMEM((length, length), F32),
            pltpu.VMEM((length, length), F32),
            dma((2,)),
            dma((PIECES,)), dma((PIECES,)),
            dma((wide_x, nk)), dma((wide_x, nk)),
            dma((PIECES,)), dma((PIECES,)),
            dma((ny, PIECES)), dma((ny, PIECES)),
            dma((near, PIECES)), dma((near, PIECES)),
            dma((2, nz, nk)), dma((nz, nk)),
            dma((nz, nk)), dma((nz + 1, nk)),
            dma((ny, nk)), dma((ny, nk)),
            dma((near, nk)), dma((near, nk)),
            dma((nk,)), dma((nk,)),
            dma((hops, nk)), dma((hops, nk)),
            dma((hops, nk)), dma((hops, nk)),
        ],
        compiler_params=pltpu.CompilerParams(
            collective_id=0, has_side_effects=True, vmem_limit_bytes=63 * 2**20
        ),
        cost_estimate=pl.CostEstimate(flops=flops, bytes_accessed=16 * 2**20, transcendentals=0),
    )(lengths, *tokens, cot, weight, *parameters)


def on_device(
    query_branch,
    key_branch,
    value_branch,
    out_cotangent,
    out_weight,
    residues,
    decay_rates,
    skip_gains,
    record_lengths,
):
    length, channels = query_branch.shape
    modes = residues.shape[1]
    nz, nx, ny = lax.axis_size("z"), lax.axis_size("x"), lax.axis_size("y")
    ctx = nz * nx
    hops = -(-(length * ctx // 4) // length)

    coeffs = residues * jnp.sqrt(1.0 - jnp.exp(-2.0 * decay_rates))
    return fused_call(
        (nz, nx, ny, hops, modes),
        record_lengths,
        (query_branch, key_branch, value_branch), out_cotangent, out_weight,
        (decay_rates, coeffs, skip_gains[None, :]),
    )


def solution(mesh):
    ctx, tp = mesh.devices.shape
    fine = Mesh(mesh.devices.reshape(tp, ctx // tp, tp // CORES, CORES), ("z", "x", "y", "c"))
    tokens = P(("z", "x"), ("y", "c"))
    placed = (
        tokens,
        tokens,
        tokens,
        tokens,
        P(("y", "c"), ("z", "x")),
        P(("y", "c"), None),
        P(("y", "c"), None),
        P(("y", "c")),
        P(),
    )
    return jax.shard_map(
        on_device,
        mesh=fine,
        in_specs=placed,
        out_specs=(tokens, tokens, tokens, tokens),
        check_vma=False,
    )
```

```python
import functools

import jax
import jax.numpy as jnp
from jax import lax
from jax.experimental import pallas as pl
from jax.experimental.pallas import tpu as pltpu
from jax.sharding import Mesh, PartitionSpec as P

GSIZE = 16
LANES = 128
TILE_GROUPS = LANES // GSIZE
CORES = 2
COLS = 256
PIECES = 4
AHEAD = 2
F32, BF16 = jnp.float32, jnp.bfloat16
MESH = pl.DeviceIdType.MESH


def split(a):
    hi = a.astype(BF16)
    return hi, (a - hi.astype(F32)).astype(BF16)


def positions(rows, length):
    return lax.broadcasted_iota(jnp.int32, (rows, length), 1).astype(F32)


def inflow_rows(rates, coeffs, pos, first):
    return coeffs * jnp.exp(-rates * (pos + 1.0)) * first


def outflow_rows(rates, pos, last):
    return jnp.exp(-rates * (pos.shape[1] - 1.0 - pos)) * last


def own_lanes(shape, group):
    lane = lax.broadcasted_iota(jnp.int32, shape, 1)
    return (lane >= group * GSIZE) & (lane < (group + 1) * GSIZE)


def weighted_state(rows, x, modes):
    hi, lo = split(rows)
    full = jnp.dot(hi, x, preferred_element_type=F32) + jnp.dot(lo, x, preferred_element_type=F32)
    state = jnp.zeros((modes, LANES), F32)
    for g in range(TILE_GROUPS):
        part = full[g * modes : (g + 1) * modes]
        state = jnp.where(own_lanes(part.shape, g), part, state)
    return state


def contract_first(a, b):
    return lax.dot_general(a, b, (((0,), (0,)), ((), ())), preferred_element_type=F32)


def from_state(rows, state, modes):
    blocks = [jnp.where(own_lanes(state.shape, g), state, 0.0) for g in range(TILE_GROUPS)]
    state_rows = jnp.concatenate(blocks, axis=0)
    r_hi, r_lo = split(rows)
    s_hi, s_lo = split(state_rows)
    return contract_first(r_hi, s_hi) + contract_first(r_lo, s_hi) + contract_first(r_hi, s_lo)


def convolve(left, right, mask, x, modes):
    l_hi, l_lo = split(left)
    r_hi, r_lo = split(right)
    total = jnp.zeros(x.shape, F32)
    for g in range(TILE_GROUPS):
        rows = slice(g * modes, (g + 1) * modes)
        a = jnp.concatenate([l_hi[rows], l_lo[rows], l_hi[rows]], axis=0)
        b = jnp.concatenate([r_hi[rows], r_hi[rows], r_lo[rows]], axis=0)
        kernel = (contract_first(a, b) * mask).astype(BF16)
        own = jnp.where(own_lanes(x.shape, g), x, jnp.zeros_like(x))
        total = total + jnp.dot(kernel, own, preferred_element_type=F32)
    return total


def when(cond):
    return pl.when(cond)


def fused(sizes, lengths, query, key, value, cot, w_hbm, rates_in, coeffs_in, skip,
          yout, qgrad, kgrad, vgrad,
          w, wg, dyg, part, sbuf, rbuf, xg, yas, yar, ybs, ybr, yp, yf, yfs, yfr, acc, mixed, fgrad, fown, fin, bown, bin_, crelay,
          rates, coeffs, first, last, mask, mask_t,
          lsem, rss, rrs, wss, wrs, css, crs, gss, grs, fss, frs, xss, xrs, dss, drs, ass, ars, bss, brs, yss, yrs,
          sfs, sfr, sbs, sbr):
    nz, nx, ny, hops, modes = sizes
    length, channels = query.shape
    width = w.shape[1]
    ctx = nz * nx
    rows = TILE_GROUPS * modes
    ring = part.shape[0]
    tiles = COLS // LANES
    nk = channels // COLS
    nw = width // COLS
    halves = PIECES
    hrows = length // halves
    z, x = lax.axis_index("z"), lax.axis_index("x")
    y, c = lax.axis_index("y"), lax.axis_index("c")
    t = y * CORES + c
    mine = c * ny + lax.rem(y - z + nz * ny, ny)
    holder = (t, x, lax.rem(z + t, ny), lax.div(z, ny))
    owner = (mine, x, lax.div(z, CORES), lax.rem(z, CORES))
    stays = (t == z) & (y == lax.rem(z + t, ny)) & (c == lax.div(z, ny))
    leaves = jnp.logical_not(stays)
    two_lines = ny == 2
    on_line = y == lax.rem(z + c, ny)
    via = (z, x, lax.rem(y + 1, ny), c)
    side_t = lax.rem(y + 1, ny) * CORES + c
    side_holder = (side_t, x, y, lax.div(z, ny))
    side_stays = on_line & (side_t == z) & (c == lax.div(z, ny))
    side_leaves = on_line & jnp.logical_not(side_stays)
    side_source = (mine, x, y, lax.rem(z, CORES))
    by_side = (y != lax.div(z, CORES)) & jnp.logical_not((mine == z) & (c == lax.rem(z, CORES)))
    if not two_lines:
        on_line = y == y
        side_stays = side_leaves = by_side = y != y
    arrives = leaves & jnp.logical_not(side_stays)
    twin = (z, x, y, 1 - c)
    index = z * nx + x

    def along(move):
        return (lax.div(index + move, nx), lax.rem(index + move, nx), y, c)

    def cp(src, dst, ssem, rsem, dev):
        return pltpu.make_async_remote_copy(
            src_ref=src, dst_ref=dst, send_sem=ssem, recv_sem=rsem, device_id=dev, device_id_type=MESH
        )

    def cols(i):
        return pl.ds(pl.multiple_of(i * COLS, COLS), COLS)

    barrier = pltpu.get_barrier_semaphore()
    for dx in range(1, nx):
        pl.semaphore_signal(barrier, 1, device_id=(z, lax.rem(x + dx, nx), y, c), device_id_type=MESH)
    for dy in range(1, ny):
        pl.semaphore_signal(barrier, 1, device_id=(z, x, lax.rem(y + dy, ny), c), device_id_type=MESH)
    pl.semaphore_signal(barrier, 1, device_id=twin, device_id_type=MESH)

    @when(z > 0)
    def _():
        pl.semaphore_signal(barrier, 1, device_id=(z - 1, x, y, c), device_id_type=MESH)

    @when(z < nz - 1)
    def _():
        pl.semaphore_signal(barrier, 1, device_id=(z + 1, x, y, c), device_id_type=MESH)

    @when(leaves)
    def _():
        pl.semaphore_signal(barrier, 1, device_id=holder, device_id_type=MESH)
        pl.semaphore_signal(barrier, 1, device_id=owner, device_id_type=MESH)

    @when(side_leaves)
    def _():
        pl.semaphore_signal(barrier, 1, device_id=side_holder, device_id_type=MESH)

    @when(by_side)
    def _():
        pl.semaphore_signal(barrier, 1, device_id=side_source, device_id_type=MESH)

    def one(cond):
        return cond.astype(jnp.int32)

    greetings = (nx - 1) + (ny - 1) + 1 + one(z > 0) + one(z < nz - 1) + 2 * one(leaves) + one(side_leaves) + one(by_side)
    for hop in range(1, hops + 1):
        for move in (hop, -hop):
            there = (index + move >= 0) & (index + move < ctx)
            greetings = greetings + one(there)

            @when(there)
            def _():
                pl.semaphore_signal(barrier, 1, device_id=along(move), device_id_type=MESH)

    base = index * length
    row_pos = lax.broadcasted_iota(jnp.int32, (1, length), 1)
    col_pos = lax.broadcasted_iota(jnp.int32, (length, 1), 0)
    row_segment, col_segment = jnp.zeros_like(row_pos), jnp.zeros_like(col_pos)
    offset, started = jnp.int32(0), jnp.int32(0)
    passed = [[index - way * hop for hop in range(1, hops + 1)] for way in (1, -1)]
    starts_in = [[jnp.int32(0)] * hops for _ in range(2)]

    def starts(block):
        return one((offset >= block * length) & (offset < block * length + length))

    for record in range(lengths.shape[0]):
        here = jnp.where(offset >= base, offset - base, length)
        row_segment += (row_pos >= here).astype(jnp.int32)
        col_segment += (col_pos >= here).astype(jnp.int32)
        started += starts(index)
        for way in range(2):
            starts_in[way] = [starts_in[way][i] + starts(passed[way][i]) for i in range(hops)]
        offset += lengths[record]

    opened = [[jnp.where(count > 0, 0.0, 1.0) for count in counts] for counts in starts_in]
    first[...] = (row_segment == 0).astype(F32)
    last[...] = (row_segment == started).astype(F32)
    together = col_segment == row_segment
    mask[...] = (together & (col_pos >= row_pos)).astype(F32)
    mask_t[...] = (together & (col_pos <= row_pos)).astype(F32)

    for source, target in ((rates_in, rates), (coeffs_in, coeffs)):
        for group in range(channels // GSIZE):
            target[group * modes : (group + 1) * modes, :] = jnp.broadcast_to(source[:, group : group + 1], (modes, LANES))

    pl.semaphore_wait(barrier, greetings)

    def w_copy(d, k):
        return cp(w_hbm.at[cols(k)], wg.at[d - 1, cols(k)], wss.at[d - 1, k], wrs.at[d - 1, k], (z, lax.rem(x + d, nx), y, c))

    def half(h):
        return pl.ds(h * hrows, hrows)

    def cot_copy(h):
        return cp(cot.at[half(h)], dyg.at[z, half(h)], css.at[h], crs.at[h], holder)

    def side_copy(h):
        return cp(cot.at[half(h)], crelay.at[half(h)], rss.at[h], rrs.at[h], via)

    def side_relay(h):
        return cp(crelay.at[half(h)], dyg.at[z, half(h)], rss.at[h], crs.at[h], side_holder)

    def cot_arrival(h):
        return cp(cot.at[half(h)], dyg.at[mine, half(h)], css.at[h], crs.at[h], holder)

    def held_by(core, d):
        return core * ny + lax.rem(y - d - z + nz * ny + ny, ny)

    def spread(d, h):
        dev = twin if d == 0 else (z, x, lax.rem(y + d, ny), c)
        return cp(dyg.at[mine, half(h)], dyg.at[mine, half(h)], gss.at[d, h], grs.at[d, h], dev)

    def spread_arrival(d, h):
        slot = held_by(1 - c if d == 0 else c, d)
        return cp(dyg.at[slot, half(h)], dyg.at[slot, half(h)], gss.at[d, h], grs.at[d, h], twin)

    def relay(d, h):
        slot = held_by(c, d)
        return cp(dyg.at[slot, half(h)], dyg.at[slot, half(h)], fss.at[d - 1, h], frs.at[d - 1, h], twin)

    def relay_arrival(d, h):
        slot = held_by(1 - c, d)
        return cp(dyg.at[slot, half(h)], dyg.at[slot, half(h)], fss.at[d - 1, h], frs.at[d - 1, h], twin)

    def x_copy(up, o, j):
        dev = (z + 1, x, y, c) if up else (z - 1, x, y, c)
        side = 0 if up else 1
        return cp(xg.at[o, :, cols(j)], xg.at[o, :, cols(j)], xss.at[side, o, j], xrs.at[o, j], dev)

    def d_copy(up, o, k):
        dev = (z + 1, x, y, c) if up else (z - 1, x, y, c)
        slot = o + 1 if up else o
        return cp(sbuf.at[o, k], rbuf.at[slot, k], dss.at[o, k], drs.at[slot, k], dev)

    def a_copy(o, q):
        slot = lax.rem(o, ny)
        return cp(yas.at[slot, :, cols(q)], yar.at[slot, :, cols(q)], ass.at[slot, q], ars.at[slot, q], twin)

    def b_copy(yd, q):
        slot = lax.rem(yd + ny - y, ny) - 1
        return cp(ybs.at[slot, :, cols(q)], ybr.at[slot, :, cols(q)], bss.at[slot, q], brs.at[slot, q], (z, x, yd, c))

    def y_copy(q):
        return cp(yfs.at[:, cols(q)], yfr.at[:, cols(q)], yss.at[q], yrs.at[q], owner)

    def f_copy(hop, j):
        return cp(fown.at[j], fin.at[hop - 1, j], sfs.at[hop - 1, j], sfr.at[hop - 1, j], along(hop))

    def s_copy(hop, j):
        return cp(bown.at[j], bin_.at[hop - 1, j], sbs.at[hop - 1, j], sbr.at[hop - 1, j], along(-hop))

    pos = positions(rows, length)

    def lanes(j, i):
        return pl.ds(pl.multiple_of(j * COLS + i * LANES, LANES), LANES)

    def parameters(ref, j, i):
        tile = ref[pl.ds(pl.multiple_of((j * tiles + i) * rows, rows), rows), :]
        return jnp.concatenate([tile] * (length // LANES), axis=1)

    def mode_rates(j, i):
        tile = rates[pl.ds(pl.multiple_of((j * tiles + i) * rows, rows), rows), :]
        result = tile[:modes]
        for g in range(1, TILE_GROUPS):
            result = jnp.where(own_lanes(result.shape, g), tile[g * modes : (g + 1) * modes], result)
        return result

    def gated_of(at):
        return (key[:, at].astype(F32) * value[:, at].astype(F32)).astype(BF16)

    def forward_state(j):
        for i in range(tiles):
            r = parameters(rates, j, i)
            fown[j, :, i * LANES : (i + 1) * LANES] = weighted_state(
                outflow_rows(r, pos, last[...]), gated_of(lanes(j, i)), modes
            )
        for hop in range(1, hops + 1):
            @when(index + hop < ctx)
            def _():
                f_copy(hop, j).start()

    def entering(j, copy, ref, sign, way):
        acc[:modes, :] = jnp.zeros((modes, COLS), F32)
        factor = jnp.ones((modes, COLS), F32)
        through = jnp.exp(-length * jnp.concatenate([mode_rates(j, i) for i in range(tiles)], axis=1))
        for hop in range(1, hops + 1):
            there = (index - hop >= 0) if sign > 0 else (index + hop < ctx)
            now = factor

            @when(there)
            def _():
                copy(hop, j).wait_recv()
                acc[:modes, :] += now * ref[hop - 1, j]

            if hop < hops:
                factor = factor * through * opened[way][hop - 1]

    def forward_filter(j):
        entering(j, f_copy, fin, 1, 0)
        for i in range(tiles):
            at = lanes(j, i)
            r, co = parameters(rates, j, i), parameters(coeffs, j, i)
            g = gated_of(at)
            half = length / 2.0
            total = convolve(co * jnp.exp(-r * (pos - half)), jnp.exp(r * (pos - half)), mask[...], g, modes)
            total = total + from_state(
                inflow_rows(r, co, pos, first[...]), acc[:modes, i * LANES : (i + 1) * LANES], modes
            )
            result = total.astype(BF16).astype(F32) + skip[:, at] * g.astype(F32)
            mixed[:, at] = result
            xg[z, :, at] = (query[:, at].astype(F32) * result).astype(BF16)

        @when(z < nz - 1)
        def _():
            x_copy(True, z, j).start()

        @when(z > 0)
        def _():
            x_copy(False, z, j).start()

    def adjoint_state(j):
        for i in range(tiles):
            at = lanes(j, i)
            r, co = parameters(rates, j, i), parameters(coeffs, j, i)
            g = acc[:, i * LANES : (i + 1) * LANES].astype(BF16).astype(F32)
            f = (g * query[:, at].astype(F32)).astype(BF16)
            fgrad[:, at] = f
            qgrad[:, at] = (g * mixed[:, at]).astype(BF16)
            bown[j, :, i * LANES : (i + 1) * LANES] = weighted_state(inflow_rows(r, co, pos, first[...]), f, modes)
        for hop in range(1, hops + 1):
            @when(index - hop >= 0)
            def _():
                s_copy(hop, j).start()

    def adjoint_filter(j):
        entering(j, s_copy, bin_, -1, 1)
        for i in range(tiles):
            at = lanes(j, i)
            r, co = parameters(rates, j, i), parameters(coeffs, j, i)
            f = fgrad[:, at]
            half = length / 2.0
            total = convolve(jnp.exp(r * (pos - half)), co * jnp.exp(-r * (pos - half)), mask_t[...], f, modes)
            total = total + from_state(
                outflow_rows(r, pos, last[...]), acc[:modes, i * LANES : (i + 1) * LANES], modes
            )
            result = total.astype(BF16).astype(F32) + skip[:, at] * f.astype(F32)
            kgrad[:, at] = (result * value[:, at].astype(F32)).astype(BF16)
            vgrad[:, at] = (result * key[:, at].astype(F32)).astype(BF16)

    own_cot = pltpu.make_async_copy(cot, dyg.at[z], lsem.at[1])
    own_w = pltpu.make_async_copy(w_hbm, w, lsem.at[0])

    def start_w(k):
        for d in range(1, nx):
            w_copy(d, k).start()

    def repeat(lo, hi, body):
        def run(j, _):
            body(j)
            return 0

        lax.fori_loop(lo, hi, run, 0)

    def valid(k):
        return (k >= 0) & (k < nk)

    def pass_on(s):
        for h in range(1, nz):
            j = s - (h - 1)
            for up in (True, False):
                o = z - h if up else z + h
                there = (o >= 0) if up else (o < nz)
                further = (z < nz - 1) if up else (z > 0)

                @when(valid(j) & there)
                def _():
                    x_copy(up, o, j).wait_recv()

                    @when(further)
                    def _():
                        x_copy(up, o, j).start()

    repeat(0, nk, forward_state)

    @when(leaves & on_line)
    def _():
        for h in range(halves):
            cot_copy(h).start()

    @when(jnp.logical_not(on_line))
    def _():
        for h in range(halves):
            side_copy(h).start()

    @when(stays)
    def _():
        own_cot.start()

    repeat(0, nk, start_w)
    own_w.start()
    repeat(0, nk // 2, forward_filter)

    if two_lines:
        @when(on_line)
        def _():
            for h in range(halves):
                side_copy(h).wait_recv()

                @when(side_leaves)
                def _():
                    side_relay(h).start()

                @when(side_stays)
                def _():
                    dyg[z, half(h)] = crelay[half(h)]

    repeat(nk // 2, nk, forward_filter)
    repeat(0, AHEAD // 2, pass_on)

    @when(stays)
    def _():
        own_cot.wait()

    for h in range(halves):
        @when(arrives)
        def _():
            cot_arrival(h).wait_recv()

        for d in range(ny):
            spread(d, h).start()

    repeat(AHEAD // 2, AHEAD, pass_on)

    for h in range(halves):
        for d in range(1, ny):
            spread_arrival(d, h).wait_recv()
            relay(d, h).start()
    own_w.wait()
    for h in range(halves):
        spread_arrival(0, h).wait_recv()
        for d in range(1, ny):
            relay_arrival(d, h).wait_recv()

    lag = jnp.maximum(z, nz - 1 - z)

    def column_of(src, i):
        return lax.rem(x + nx - src, nx) * nw + i

    def project(src, o):
        slot, core = lax.rem(o, ny), lax.div(o, ny)

        def column(i, _):
            q = column_of(src, i)
            ref = w if src == 0 else wg.at[src - 1]
            p = jnp.dot(xg[o], ref[:, cols(i)], preferred_element_type=F32)

            @when(c != core)
            def _():
                yas[slot, :, cols(q)] = p.astype(BF16)
                a_copy(o, q).start()

            @when(c == core)
            def _():
                yp[slot, :, cols(q)] = p

            return 0

        lax.fori_loop(0, nw, column, 0)

    def sum_cores(src, o):
        slot, core = lax.rem(o, ny), lax.div(o, ny)
        yd = lax.rem(o + z, ny)

        @when(c == core)
        def _():
            def add(i, _):
                q = column_of(src, i)
                a_copy(o, q).wait_recv()
                total = yp[slot, :, cols(q)] + yar[slot, :, cols(q)].astype(F32)

                @when(yd != y)
                def _():
                    ybs[lax.rem(yd + ny - y, ny) - 1, :, cols(q)] = total.astype(BF16)
                    b_copy(yd, q).start()

                @when(yd == y)
                def _():
                    yf[:, cols(q)] = total

                return 0

            lax.fori_loop(0, nw, add, 0)

    def blocks(work, src, h):
        def side(i, _):
            o = z + h * (1 - 2 * i)

            @when((o >= 0) & (o < nz) & ((h > 0) | (i == 0)))
            def _():
                work(src, o)

            return 0

        lax.fori_loop(0, 2, side, 0)

    def finish(src):
        def last_sum(i, _):
            q = column_of(src, i)
            total = yf[:, cols(q)]
            for d in range(1, ny):
                cp(ybs.at[d - 1, :, cols(q)], ybr.at[d - 1, :, cols(q)], bss.at[d - 1, q], brs.at[d - 1, q], twin).wait_recv()
                total = total + ybr[d - 1, :, cols(q)].astype(F32)

            yfs[:, cols(q)] = total.astype(BF16)

            @when(leaves)
            def _():
                y_copy(q).start()

            return 0

        lax.fori_loop(0, nw, last_sum, 0)

    distance = jnp.maximum(mine - z, z - mine)

    def step(s, _):
        k = s - AHEAD

        @when(k < nk)
        def _():
            for d in range(1, nx):
                w_copy(d, k).wait_recv()
            own_cols = pl.ds(pl.multiple_of(x * width, LANES), width)

            def rows_of(o, _):
                total = lax.dot_general(
                    dyg[o, :, own_cols], w[cols(k), :], (((1,), (1,)), ((), ())), preferred_element_type=F32
                )
                for d in range(1, nx):
                    from_cols = pl.ds(pl.multiple_of(lax.rem(x + nx - d, nx) * width, LANES), width)
                    total = total + lax.dot_general(
                        dyg[o, :, from_cols], wg[d - 1, cols(k), :], (((1,), (1,)), ((), ())), preferred_element_type=F32
                    )
                part[lax.rem(k, ring), o] = total
                return 0

            lax.fori_loop(0, nz, rows_of, 0)

        up_k = k - z

        @when(valid(up_k) & (z < nz - 1))
        def _():
            for o in range(nz - 1, 0, -1):
                @when(o > z)
                def _():
                    @when(z > 0)
                    def _():
                        d_copy(True, o, up_k).wait_recv()
                        sbuf[o, up_k] = (part[lax.rem(up_k, ring), o] + rbuf[o + 1, up_k].astype(F32)).astype(BF16)

                    @when(z == 0)
                    def _():
                        sbuf[o, up_k] = part[lax.rem(up_k, ring), o].astype(BF16)

                    d_copy(True, o, up_k).start()

        down_k = k - (nz - 1 - z)

        @when(valid(down_k) & (z > 0))
        def _():
            for o in range(nz - 1):
                @when(o < z)
                def _():
                    @when(z < nz - 1)
                    def _():
                        d_copy(False, o, down_k).wait_recv()
                        sbuf[o, down_k] = (part[lax.rem(down_k, ring), o] + rbuf[o, down_k].astype(F32)).astype(BF16)

                    @when(z == nz - 1)
                    def _():
                        sbuf[o, down_k] = part[lax.rem(down_k, ring), o].astype(BF16)

                    d_copy(False, o, down_k).start()

        pass_on(s)

        h = s - nk + 1

        @when((h >= 0) & (h < nz))
        def _():
            blocks(project, 0, h)
            blocks(sum_cores, 0, h)

        @when(k == nk)
        def _():
            for work in (project, sum_cores):
                def near(h, _):
                    for src in range(1, nx):
                        blocks(work, src, h)
                    return 0

                lax.fori_loop(0, min(nz, AHEAD + 3), near, 0)

        if AHEAD + 3 < nz:
            @when((k > nk) & (s - nk + 2 < nz))
            def _():
                for src in range(1, nx):
                    blocks(project, src, s - nk + 2)
                    blocks(sum_cores, src, s - nk + 2)

        @when(s == nk + 0 + distance)
        def _():
            finish(0)

        @when(k == nk + 1 + jnp.maximum(distance - AHEAD - 2, 0))
        def _():
            for src in range(1, nx):
                finish(src)

        own_k = k - lag

        @when(valid(own_k))
        def _():
            acc[...] = part[lax.rem(own_k, ring), z]

            @when(z > 0)
            def _():
                d_copy(True, z, own_k).wait_recv()
                acc[...] += rbuf[z + 1, own_k].astype(F32)

            @when(z < nz - 1)
            def _():
                d_copy(False, z, own_k).wait_recv()
                acc[...] += rbuf[z, own_k].astype(F32)

            adjoint_state(own_k)

        far_k = k - nz - 1

        @when(valid(far_k))
        def _():
            adjoint_filter(far_k)

        return 0

    lax.fori_loop(AHEAD, AHEAD + nk + nz + 1, step, 0)

    @when(stays)
    def _():
        yout[...] = yfs[...]

    @when(leaves)
    def _():
        def land(q, _):
            y_copy(q).wait()
            return 0

        lax.fori_loop(0, nk, land, 0)
        yout[...] = yfr[...]

    @when(leaves & on_line)
    def _():
        for h in range(halves):
            cot_copy(h).wait_send()

    @when(jnp.logical_not(on_line))
    def _():
        for h in range(halves):
            side_copy(h).wait_send()

    @when(side_leaves)
    def _():
        for h in range(halves):
            side_relay(h).wait_send()

    for h in range(halves):
        for d in range(ny):
            spread(d, h).wait_send()
        for d in range(1, ny):
            relay(d, h).wait_send()

    def drain(k, _):
        for d in range(1, nx):
            w_copy(d, k).wait_send()
        for slot in range(ny):
            a_copy((1 - c) * ny + slot, k).wait_send()
        for d in range(1, ny):
            b_copy(lax.rem(y + d, ny), k).wait_send()
        for o in range(nz):
            @when((z < nz - 1) & (o <= z))
            def _():
                x_copy(True, o, k).wait_send()

            @when((z > 0) & (o >= z))
            def _():
                x_copy(False, o, k).wait_send()

            @when(o > z)
            def _():
                d_copy(True, o, k).wait_send()

            @when(o < z)
            def _():
                d_copy(False, o, k).wait_send()

        for hop in range(1, hops + 1):
            @when(index + hop < ctx)
            def _():
                f_copy(hop, k).wait_send()

            @when(index - hop >= 0)
            def _():
                s_copy(hop, k).wait_send()

        return 0

    lax.fori_loop(0, nk, drain, 0)


def fused_call(sizes, lengths, tokens, cot, weight, parameters):
    nz, nx, ny, hops, modes = sizes
    length, channels = cot.shape
    width = weight.shape[1]
    nk = channels // COLS
    vmem = pl.BlockSpec(memory_space=pltpu.VMEM)
    hbm = pl.BlockSpec(memory_space=pl.ANY)
    token = jax.ShapeDtypeStruct((length, channels), BF16)
    dma = pltpu.SemaphoreType.DMA
    near = max(ny - 1, 1)
    wide_x = max(nx - 1, 1)
    flops = 8 * nz * length * channels * width * nx // 2
    return pl.pallas_call(
        functools.partial(fused, sizes),
        out_shape=(token,) * 4,
        in_specs=[pl.BlockSpec(memory_space=pltpu.SMEM)] + [vmem] * 3 + [hbm] * 2 + [vmem] * len(parameters),
        out_specs=(vmem,) * 4,
        scratch_shapes=[
            pltpu.VMEM((channels, width), BF16),
            pltpu.VMEM((wide_x, channels, width), BF16),
            pltpu.VMEM((nz, length, channels), BF16),
            pltpu.VMEM((nz, nz, length, COLS), F32),
            pltpu.VMEM((nz, nk, length, COLS), BF16),
            pltpu.VMEM((nz + 1, nk, length, COLS), BF16),
            pltpu.VMEM((nz, length, channels), BF16),
            pltpu.VMEM((ny, length, channels), BF16),
            pltpu.VMEM((ny, length, channels), BF16),
            pltpu.VMEM((near, length, channels), BF16),
            pltpu.VMEM((near, length, channels), BF16),
            pltpu.VMEM((ny, length, channels), F32),
            pltpu.VMEM((length, channels), F32),
            pltpu.VMEM((length, channels), BF16),
            pltpu.VMEM((length, channels), BF16),
            pltpu.VMEM((length, COLS), F32),
            pltpu.VMEM((length, channels), F32),
            pltpu.VMEM((length, channels), BF16),
            pltpu.VMEM((nk, modes, COLS), F32),
            pltpu.VMEM((hops, nk, modes, COLS), F32),
            pltpu.VMEM((nk, modes, COLS), F32),
            pltpu.VMEM((hops, nk, modes, COLS), F32),
            pltpu.VMEM((length, channels), BF16),
            pltpu.VMEM((channels // GSIZE * modes, LANES), F32),
            pltpu.VMEM((channels // GSIZE * modes, LANES), F32),
            pltpu.VMEM((1, length), F32),
            pltpu.VMEM((1, length), F32),
            pltpu.VMEM((length, length), F32),
            pltpu.VMEM((length, length), F32),
            dma((2,)),
            dma((PIECES,)), dma((PIECES,)),
            dma((wide_x, nk)), dma((wide_x, nk)),
            dma((PIECES,)), dma((PIECES,)),
            dma((ny, PIECES)), dma((ny, PIECES)),
            dma((near, PIECES)), dma((near, PIECES)),
            dma((2, nz, nk)), dma((nz, nk)),
            dma((nz, nk)), dma((nz + 1, nk)),
            dma((ny, nk)), dma((ny, nk)),
            dma((near, nk)), dma((near, nk)),
            dma((nk,)), dma((nk,)),
            dma((hops, nk)), dma((hops, nk)),
            dma((hops, nk)), dma((hops, nk)),
        ],
        compiler_params=pltpu.CompilerParams(
            collective_id=0, has_side_effects=True, vmem_limit_bytes=63 * 2**20
        ),
        cost_estimate=pl.CostEstimate(flops=flops, bytes_accessed=16 * 2**20, transcendentals=0),
    )(lengths, *tokens, cot, weight, *parameters)


def hand_over(results):
    count = len(results)
    length, channels = results[0].shape
    steps = 4

    def kernel(*refs):
        for i in range(count):
            refs[count + i][...] = refs[i][...]

    block = pl.BlockSpec((length // steps, channels), lambda i: (i, 0))
    size = sum(r.size * 2 for r in results)
    return pl.pallas_call(
        kernel,
        grid=(steps,),
        out_shape=tuple(jax.ShapeDtypeStruct(r.shape, r.dtype) for r in results),
        in_specs=[block] * count,
        out_specs=(block,) * count,
        cost_estimate=pl.CostEstimate(flops=0, bytes_accessed=2 * size, transcendentals=0),
    )(*results)


def on_device(
    query_branch,
    key_branch,
    value_branch,
    out_cotangent,
    out_weight,
    residues,
    decay_rates,
    skip_gains,
    record_lengths,
):
    length, channels = query_branch.shape
    modes = residues.shape[1]
    nz, nx, ny = lax.axis_size("z"), lax.axis_size("x"), lax.axis_size("y")
    ctx = nz * nx
    hops = -(-(length * ctx // 4) // length)

    rates = decay_rates.T
    coeffs = residues.T * jnp.sqrt(1.0 - jnp.exp(-2.0 * rates))
    results = fused_call(
        (nz, nx, ny, hops, modes),
        record_lengths,
        (query_branch, key_branch, value_branch), out_cotangent, out_weight,
        (rates, coeffs, skip_gains[None, :]),
    )
    return hand_over(results)


def solution(mesh):
    ctx, tp = mesh.devices.shape
    fine = Mesh(mesh.devices.reshape(tp, ctx // tp, tp // CORES, CORES), ("z", "x", "y", "c"))
    tokens = P(("z", "x"), ("y", "c"))
    placed = (
        tokens,
        tokens,
        tokens,
        tokens,
        P(("y", "c"), ("z", "x")),
        P(("y", "c"), None),
        P(("y", "c"), None),
        P(("y", "c")),
        P(),
    )
    return jax.shard_map(
        on_device,
        mesh=fine,
        in_specs=placed,
        out_specs=(tokens, tokens, tokens, tokens),
        check_vma=False,
    )
```

```python
import functools

import jax
import jax.numpy as jnp
from jax import lax
from jax.experimental import pallas as pl
from jax.experimental.pallas import tpu as pltpu
from jax.sharding import Mesh, PartitionSpec as P

GSIZE = 16
LANES = 128
TILE_GROUPS = LANES // GSIZE
CORES = 2
COLS = 256
PIECES = 4
AHEAD = 2
F32, BF16 = jnp.float32, jnp.bfloat16
MESH = pl.DeviceIdType.MESH


def split(a):
    hi = a.astype(BF16)
    return hi, (a - hi.astype(F32)).astype(BF16)


def positions(rows, length):
    return lax.broadcasted_iota(jnp.int32, (rows, length), 1).astype(F32)


def inflow_rows(rates, coeffs, pos, first):
    return coeffs * jnp.exp(-rates * (pos + 1.0)) * first


def outflow_rows(rates, pos, last):
    return jnp.exp(-rates * (pos.shape[1] - 1.0 - pos)) * last


def own_lanes(shape, group):
    lane = lax.broadcasted_iota(jnp.int32, shape, 1)
    return (lane >= group * GSIZE) & (lane < (group + 1) * GSIZE)


def weighted_state(rows, x, modes):
    hi, lo = split(rows)
    full = jnp.dot(hi, x, preferred_element_type=F32) + jnp.dot(lo, x, preferred_element_type=F32)
    state = jnp.zeros((modes, LANES), F32)
    for g in range(TILE_GROUPS):
        part = full[g * modes : (g + 1) * modes]
        state = jnp.where(own_lanes(part.shape, g), part, state)
    return state


def contract_first(a, b):
    return lax.dot_general(a, b, (((0,), (0,)), ((), ())), preferred_element_type=F32)


def from_state(rows, state, modes):
    blocks = [jnp.where(own_lanes(state.shape, g), state, 0.0) for g in range(TILE_GROUPS)]
    state_rows = jnp.concatenate(blocks, axis=0)
    r_hi, r_lo = split(rows)
    s_hi, s_lo = split(state_rows)
    return contract_first(r_hi, s_hi) + contract_first(r_lo, s_hi) + contract_first(r_hi, s_lo)


def convolve(left, right, mask, x, modes):
    l_hi, l_lo = split(left)
    r_hi, r_lo = split(right)
    total = jnp.zeros(x.shape, F32)
    for g in range(TILE_GROUPS):
        rows = slice(g * modes, (g + 1) * modes)
        a = jnp.concatenate([l_hi[rows], l_lo[rows], l_hi[rows]], axis=0)
        b = jnp.concatenate([r_hi[rows], r_hi[rows], r_lo[rows]], axis=0)
        kernel = (contract_first(a, b) * mask).astype(BF16)
        own = jnp.where(own_lanes(x.shape, g), x, jnp.zeros_like(x))
        total = total + jnp.dot(kernel, own, preferred_element_type=F32)
    return total


def when(cond):
    return pl.when(cond)


def fused(sizes, lengths, query, key, value, cot, w_hbm, rates_in, coeffs_in, skip,
          yout, qgrad, kgrad, vgrad,
          w, wg, dyg, part, sbuf, rbuf, xg, yas, yar, ybs, ybr, yp, yf, yfs, yfr, acc, mixed, fgrad, fown, fin, bown, bin_, crelay,
          rates, coeffs, first, last, mask, mask_t,
          lsem, rss, rrs, wss, wrs, css, crs, gss, grs, fss, frs, xss, xrs, dss, drs, ass, ars, bss, brs, yss, yrs,
          sfs, sfr, sbs, sbr):
    nz, nx, ny, hops, modes = sizes
    length, channels = query.shape
    width = w.shape[1]
    ctx = nz * nx
    rows = TILE_GROUPS * modes
    ring = part.shape[0]
    tiles = COLS // LANES
    nk = channels // COLS
    nw = width // COLS
    halves = PIECES
    hrows = length // halves
    z, x = lax.axis_index("z"), lax.axis_index("x")
    y, c = lax.axis_index("y"), lax.axis_index("c")
    t = y * CORES + c
    mine = c * ny + lax.rem(y - z + nz * ny, ny)
    holder = (t, x, lax.rem(z + t, ny), lax.div(z, ny))
    owner = (mine, x, lax.div(z, CORES), lax.rem(z, CORES))
    stays = (t == z) & (y == lax.rem(z + t, ny)) & (c == lax.div(z, ny))
    leaves = jnp.logical_not(stays)
    two_lines = ny == 2
    on_line = y == lax.rem(z + c, ny)
    via = (z, x, lax.rem(y + 1, ny), c)
    side_t = lax.rem(y + 1, ny) * CORES + c
    side_holder = (side_t, x, y, lax.div(z, ny))
    side_stays = on_line & (side_t == z) & (c == lax.div(z, ny))
    side_leaves = on_line & jnp.logical_not(side_stays)
    side_source = (mine, x, y, lax.rem(z, CORES))
    by_side = (y != lax.div(z, CORES)) & jnp.logical_not((mine == z) & (c == lax.rem(z, CORES)))
    if not two_lines:
        on_line = y == y
        side_stays = side_leaves = by_side = y != y
    arrives = leaves & jnp.logical_not(side_stays)
    twin = (z, x, y, 1 - c)
    index = z * nx + x

    def along(move):
        return (lax.div(index + move, nx), lax.rem(index + move, nx), y, c)

    def cp(src, dst, ssem, rsem, dev):
        return pltpu.make_async_remote_copy(
            src_ref=src, dst_ref=dst, send_sem=ssem, recv_sem=rsem, device_id=dev, device_id_type=MESH
        )

    def cols(i):
        return pl.ds(pl.multiple_of(i * COLS, COLS), COLS)

    barrier = pltpu.get_barrier_semaphore()
    for dx in range(1, nx):
        pl.semaphore_signal(barrier, 1, device_id=(z, lax.rem(x + dx, nx), y, c), device_id_type=MESH)
    for dy in range(1, ny):
        pl.semaphore_signal(barrier, 1, device_id=(z, x, lax.rem(y + dy, ny), c), device_id_type=MESH)
    pl.semaphore_signal(barrier, 1, device_id=twin, device_id_type=MESH)

    @when(z > 0)
    def _():
        pl.semaphore_signal(barrier, 1, device_id=(z - 1, x, y, c), device_id_type=MESH)

    @when(z < nz - 1)
    def _():
        pl.semaphore_signal(barrier, 1, device_id=(z + 1, x, y, c), device_id_type=MESH)

    @when(leaves)
    def _():
        pl.semaphore_signal(barrier, 1, device_id=holder, device_id_type=MESH)
        pl.semaphore_signal(barrier, 1, device_id=owner, device_id_type=MESH)

    @when(side_leaves)
    def _():
        pl.semaphore_signal(barrier, 1, device_id=side_holder, device_id_type=MESH)

    @when(by_side)
    def _():
        pl.semaphore_signal(barrier, 1, device_id=side_source, device_id_type=MESH)

    def one(cond):
        return cond.astype(jnp.int32)

    greetings = (nx - 1) + (ny - 1) + 1 + one(z > 0) + one(z < nz - 1) + 2 * one(leaves) + one(side_leaves) + one(by_side)
    for hop in range(1, hops + 1):
        for move in (hop, -hop):
            there = (index + move >= 0) & (index + move < ctx)
            greetings = greetings + one(there)

            @when(there)
            def _():
                pl.semaphore_signal(barrier, 1, device_id=along(move), device_id_type=MESH)

    base = index * length
    row_pos = lax.broadcasted_iota(jnp.int32, (1, length), 1)
    col_pos = lax.broadcasted_iota(jnp.int32, (length, 1), 0)
    row_segment, col_segment = jnp.zeros_like(row_pos), jnp.zeros_like(col_pos)
    offset, started = jnp.int32(0), jnp.int32(0)
    passed = [[index - way * hop for hop in range(1, hops + 1)] for way in (1, -1)]
    starts_in = [[jnp.int32(0)] * hops for _ in range(2)]

    def starts(block):
        return one((offset >= block * length) & (offset < block * length + length))

    for record in range(lengths.shape[0]):
        here = jnp.where(offset >= base, offset - base, length)
        row_segment += (row_pos >= here).astype(jnp.int32)
        col_segment += (col_pos >= here).astype(jnp.int32)
        started += starts(index)
        for way in range(2):
            starts_in[way] = [starts_in[way][i] + starts(passed[way][i]) for i in range(hops)]
        offset += lengths[record]

    opened = [[jnp.where(count > 0, 0.0, 1.0) for count in counts] for counts in starts_in]
    first[...] = (row_segment == 0).astype(F32)
    last[...] = (row_segment == started).astype(F32)
    together = col_segment == row_segment
    mask[...] = (together & (col_pos >= row_pos)).astype(F32)
    mask_t[...] = (together & (col_pos <= row_pos)).astype(F32)

    for source, target in ((rates_in, rates), (coeffs_in, coeffs)):
        for group in range(channels // GSIZE):
            target[group * modes : (group + 1) * modes, :] = jnp.broadcast_to(source[:, group : group + 1], (modes, LANES))

    pl.semaphore_wait(barrier, greetings)

    def w_copy(d, k):
        return cp(w_hbm.at[cols(k)], wg.at[d - 1, cols(k)], wss.at[d - 1, k], wrs.at[d - 1, k], (z, lax.rem(x + d, nx), y, c))

    def half(h):
        return pl.ds(h * hrows, hrows)

    def cot_copy(h):
        return cp(cot.at[half(h)], dyg.at[z, half(h)], css.at[h], crs.at[h], holder)

    def side_copy(h):
        return cp(cot.at[half(h)], crelay.at[half(h)], rss.at[h], rrs.at[h], via)

    def side_relay(h):
        return cp(crelay.at[half(h)], dyg.at[z, half(h)], rss.at[h], crs.at[h], side_holder)

    def cot_arrival(h):
        return cp(cot.at[half(h)], dyg.at[mine, half(h)], css.at[h], crs.at[h], holder)

    def held_by(core, d):
        return core * ny + lax.rem(y - d - z + nz * ny + ny, ny)

    def spread(d, h):
        dev = twin if d == 0 else (z, x, lax.rem(y + d, ny), c)
        return cp(dyg.at[mine, half(h)], dyg.at[mine, half(h)], gss.at[d, h], grs.at[d, h], dev)

    def spread_arrival(d, h):
        slot = held_by(1 - c if d == 0 else c, d)
        return cp(dyg.at[slot, half(h)], dyg.at[slot, half(h)], gss.at[d, h], grs.at[d, h], twin)

    def relay(d, h):
        slot = held_by(c, d)
        return cp(dyg.at[slot, half(h)], dyg.at[slot, half(h)], fss.at[d - 1, h], frs.at[d - 1, h], twin)

    def relay_arrival(d, h):
        slot = held_by(1 - c, d)
        return cp(dyg.at[slot, half(h)], dyg.at[slot, half(h)], fss.at[d - 1, h], frs.at[d - 1, h], twin)

    def x_copy(up, o, j):
        dev = (z + 1, x, y, c) if up else (z - 1, x, y, c)
        side = 0 if up else 1
        return cp(xg.at[o, :, cols(j)], xg.at[o, :, cols(j)], xss.at[side, o, j], xrs.at[o, j], dev)

    def d_copy(up, o, k):
        dev = (z + 1, x, y, c) if up else (z - 1, x, y, c)
        slot = o + 1 if up else o
        return cp(sbuf.at[o, k], rbuf.at[slot, k], dss.at[o, k], drs.at[slot, k], dev)

    def a_copy(o, q):
        slot = lax.rem(o, ny)
        return cp(yas.at[slot, :, cols(q)], yar.at[slot, :, cols(q)], ass.at[slot, q], ars.at[slot, q], twin)

    def b_copy(yd, q):
        slot = lax.rem(yd + ny - y, ny) - 1
        return cp(ybs.at[slot, :, cols(q)], ybr.at[slot, :, cols(q)], bss.at[slot, q], brs.at[slot, q], (z, x, yd, c))

    def y_copy(q):
        return cp(yfs.at[:, cols(q)], yfr.at[:, cols(q)], yss.at[q], yrs.at[q], owner)

    def f_copy(hop, j):
        return cp(fown.at[j], fin.at[hop - 1, j], sfs.at[hop - 1, j], sfr.at[hop - 1, j], along(hop))

    def s_copy(hop, j):
        return cp(bown.at[j], bin_.at[hop - 1, j], sbs.at[hop - 1, j], sbr.at[hop - 1, j], along(-hop))

    pos = positions(rows, length)

    def lanes(j, i):
        return pl.ds(pl.multiple_of(j * COLS + i * LANES, LANES), LANES)

    def parameters(ref, j, i):
        tile = ref[pl.ds(pl.multiple_of((j * tiles + i) * rows, rows), rows), :]
        return jnp.concatenate([tile] * (length // LANES), axis=1)

    def mode_rates(j, i):
        tile = rates[pl.ds(pl.multiple_of((j * tiles + i) * rows, rows), rows), :]
        result = tile[:modes]
        for g in range(1, TILE_GROUPS):
            result = jnp.where(own_lanes(result.shape, g), tile[g * modes : (g + 1) * modes], result)
        return result

    def gated_of(at):
        return (key[:, at].astype(F32) * value[:, at].astype(F32)).astype(BF16)

    def forward_state(j):
        for i in range(tiles):
            r = parameters(rates, j, i)
            fown[j, :, i * LANES : (i + 1) * LANES] = weighted_state(
                outflow_rows(r, pos, last[...]), gated_of(lanes(j, i)), modes
            )
        for hop in range(1, hops + 1):
            @when(index + hop < ctx)
            def _():
                f_copy(hop, j).start()

    def entering(j, copy, ref, sign, way):
        acc[:modes, :] = jnp.zeros((modes, COLS), F32)
        factor = jnp.ones((modes, COLS), F32)
        through = jnp.exp(-length * jnp.concatenate([mode_rates(j, i) for i in range(tiles)], axis=1))
        for hop in range(1, hops + 1):
            there = (index - hop >= 0) if sign > 0 else (index + hop < ctx)
            now = factor

            @when(there)
            def _():
                copy(hop, j).wait_recv()
                acc[:modes, :] += now * ref[hop - 1, j]

            if hop < hops:
                factor = factor * through * opened[way][hop - 1]

    def forward_filter(j):
        entering(j, f_copy, fin, 1, 0)
        for i in range(tiles):
            at = lanes(j, i)
            r, co = parameters(rates, j, i), parameters(coeffs, j, i)
            g = gated_of(at)
            half = length / 2.0
            total = convolve(co * jnp.exp(-r * (pos - half)), jnp.exp(r * (pos - half)), mask[...], g, modes)
            total = total + from_state(
                inflow_rows(r, co, pos, first[...]), acc[:modes, i * LANES : (i + 1) * LANES], modes
            )
            result = total.astype(BF16).astype(F32) + skip[:, at] * g.astype(F32)
            mixed[:, at] = result
            xg[z, :, at] = (query[:, at].astype(F32) * result).astype(BF16)

        @when(z < nz - 1)
        def _():
            x_copy(True, z, j).start()

        @when(z > 0)
        def _():
            x_copy(False, z, j).start()

    def adjoint_state(j):
        for i in range(tiles):
            at = lanes(j, i)
            r, co = parameters(rates, j, i), parameters(coeffs, j, i)
            g = acc[:, i * LANES : (i + 1) * LANES].astype(BF16).astype(F32)
            f = (g * query[:, at].astype(F32)).astype(BF16)
            fgrad[:, at] = f
            qgrad[:, at] = (g * mixed[:, at]).astype(BF16)
            bown[j, :, i * LANES : (i + 1) * LANES] = weighted_state(inflow_rows(r, co, pos, first[...]), f, modes)
        for hop in range(1, hops + 1):
            @when(index - hop >= 0)
            def _():
                s_copy(hop, j).start()

    def adjoint_filter(j):
        entering(j, s_copy, bin_, -1, 1)
        for i in range(tiles):
            at = lanes(j, i)
            r, co = parameters(rates, j, i), parameters(coeffs, j, i)
            f = fgrad[:, at]
            half = length / 2.0
            total = convolve(jnp.exp(r * (pos - half)), co * jnp.exp(-r * (pos - half)), mask_t[...], f, modes)
            total = total + from_state(
                outflow_rows(r, pos, last[...]), acc[:modes, i * LANES : (i + 1) * LANES], modes
            )
            result = total.astype(BF16).astype(F32) + skip[:, at] * f.astype(F32)
            kgrad[:, at] = (result * value[:, at].astype(F32)).astype(BF16)
            vgrad[:, at] = (result * key[:, at].astype(F32)).astype(BF16)

    own_cot = pltpu.make_async_copy(cot, dyg.at[z], lsem.at[1])
    own_w = pltpu.make_async_copy(w_hbm, w, lsem.at[0])

    def start_w(k):
        for d in range(1, nx):
            w_copy(d, k).start()

    def repeat(lo, hi, body):
        def run(j, _):
            body(j)
            return 0

        lax.fori_loop(lo, hi, run, 0)

    def valid(k):
        return (k >= 0) & (k < nk)

    def pass_on(s):
        for h in range(1, nz):
            j = s - (h - 1)
            for up in (True, False):
                o = z - h if up else z + h
                there = (o >= 0) if up else (o < nz)
                further = (z < nz - 1) if up else (z > 0)

                @when(valid(j) & there)
                def _():
                    x_copy(up, o, j).wait_recv()

                    @when(further)
                    def _():
                        x_copy(up, o, j).start()

    repeat(0, nk, forward_state)

    @when(leaves & on_line)
    def _():
        for h in range(halves):
            cot_copy(h).start()

    @when(jnp.logical_not(on_line))
    def _():
        for h in range(halves):
            side_copy(h).start()

    @when(stays)
    def _():
        own_cot.start()

    repeat(0, nk, start_w)
    own_w.start()
    repeat(0, nk // 2, forward_filter)

    if two_lines:
        @when(on_line)
        def _():
            for h in range(halves):
                side_copy(h).wait_recv()

                @when(side_leaves)
                def _():
                    side_relay(h).start()

                @when(side_stays)
                def _():
                    dyg[z, half(h)] = crelay[half(h)]

    repeat(nk // 2, nk, forward_filter)
    repeat(0, AHEAD // 2, pass_on)

    @when(stays)
    def _():
        own_cot.wait()

    for h in range(halves):
        @when(arrives)
        def _():
            cot_arrival(h).wait_recv()

        for d in range(ny):
            spread(d, h).start()

    repeat(AHEAD // 2, AHEAD, pass_on)

    for h in range(halves):
        for d in range(1, ny):
            spread_arrival(d, h).wait_recv()
            relay(d, h).start()
    own_w.wait()
    for h in range(halves):
        spread_arrival(0, h).wait_recv()
        for d in range(1, ny):
            relay_arrival(d, h).wait_recv()

    lag = jnp.maximum(z, nz - 1 - z)

    def column_of(src, i):
        return lax.rem(x + nx - src, nx) * nw + i

    def project(src, o):
        slot, core = lax.rem(o, ny), lax.div(o, ny)

        def column(i, _):
            q = column_of(src, i)
            ref = w if src == 0 else wg.at[src - 1]
            p = jnp.dot(xg[o], ref[:, cols(i)], preferred_element_type=F32)

            @when(c != core)
            def _():
                yas[slot, :, cols(q)] = p.astype(BF16)
                a_copy(o, q).start()

            @when(c == core)
            def _():
                yp[slot, :, cols(q)] = p

            return 0

        lax.fori_loop(0, nw, column, 0)

    def sum_cores(src, o):
        slot, core = lax.rem(o, ny), lax.div(o, ny)
        yd = lax.rem(o + z, ny)

        @when(c == core)
        def _():
            def add(i, _):
                q = column_of(src, i)
                a_copy(o, q).wait_recv()
                total = yp[slot, :, cols(q)] + yar[slot, :, cols(q)].astype(F32)

                @when(yd != y)
                def _():
                    ybs[lax.rem(yd + ny - y, ny) - 1, :, cols(q)] = total.astype(BF16)
                    b_copy(yd, q).start()

                @when(yd == y)
                def _():
                    yf[:, cols(q)] = total

                return 0

            lax.fori_loop(0, nw, add, 0)

    def blocks(work, src, h):
        def side(i, _):
            o = z + h * (1 - 2 * i)

            @when((o >= 0) & (o < nz) & ((h > 0) | (i == 0)))
            def _():
                work(src, o)

            return 0

        lax.fori_loop(0, 2, side, 0)

    def finish(src):
        def last_sum(i, _):
            q = column_of(src, i)
            total = yf[:, cols(q)]
            for d in range(1, ny):
                cp(ybs.at[d - 1, :, cols(q)], ybr.at[d - 1, :, cols(q)], bss.at[d - 1, q], brs.at[d - 1, q], twin).wait_recv()
                total = total + ybr[d - 1, :, cols(q)].astype(F32)

            yfs[:, cols(q)] = total.astype(BF16)

            @when(leaves)
            def _():
                y_copy(q).start()

            return 0

        lax.fori_loop(0, nw, last_sum, 0)

    distance = jnp.maximum(mine - z, z - mine)

    def step(s, _):
        k = s - AHEAD

        @when(k < nk)
        def _():
            for d in range(1, nx):
                w_copy(d, k).wait_recv()
            own_cols = pl.ds(pl.multiple_of(x * width, LANES), width)

            def rows_of(o, _):
                total = lax.dot_general(
                    dyg[o, :, own_cols], w[cols(k), :], (((1,), (1,)), ((), ())), preferred_element_type=F32
                )
                for d in range(1, nx):
                    from_cols = pl.ds(pl.multiple_of(lax.rem(x + nx - d, nx) * width, LANES), width)
                    total = total + lax.dot_general(
                        dyg[o, :, from_cols], wg[d - 1, cols(k), :], (((1,), (1,)), ((), ())), preferred_element_type=F32
                    )
                part[lax.rem(k, ring), o] = total
                return 0

            lax.fori_loop(0, nz, rows_of, 0)

        up_k = k - z

        @when(valid(up_k) & (z < nz - 1))
        def _():
            for o in range(nz - 1, 0, -1):
                @when(o > z)
                def _():
                    @when(z > 0)
                    def _():
                        d_copy(True, o, up_k).wait_recv()
                        sbuf[o, up_k] = (part[lax.rem(up_k, ring), o] + rbuf[o + 1, up_k].astype(F32)).astype(BF16)

                    @when(z == 0)
                    def _():
                        sbuf[o, up_k] = part[lax.rem(up_k, ring), o].astype(BF16)

                    d_copy(True, o, up_k).start()

        down_k = k - (nz - 1 - z)

        @when(valid(down_k) & (z > 0))
        def _():
            for o in range(nz - 1):
                @when(o < z)
                def _():
                    @when(z < nz - 1)
                    def _():
                        d_copy(False, o, down_k).wait_recv()
                        sbuf[o, down_k] = (part[lax.rem(down_k, ring), o] + rbuf[o, down_k].astype(F32)).astype(BF16)

                    @when(z == nz - 1)
                    def _():
                        sbuf[o, down_k] = part[lax.rem(down_k, ring), o].astype(BF16)

                    d_copy(False, o, down_k).start()

        pass_on(s)

        own_k = k - lag

        @when(valid(own_k))
        def _():
            acc[...] = part[lax.rem(own_k, ring), z]

            @when(z > 0)
            def _():
                d_copy(True, z, own_k).wait_recv()
                acc[...] += rbuf[z + 1, own_k].astype(F32)

            @when(z < nz - 1)
            def _():
                d_copy(False, z, own_k).wait_recv()
                acc[...] += rbuf[z, own_k].astype(F32)

            adjoint_state(own_k)

        h = s - nk + 1

        @when((h >= 0) & (h < nz))
        def _():
            blocks(project, 0, h)
            blocks(sum_cores, 0, h)

        @when(k == nk)
        def _():
            for work in (project, sum_cores):
                def near(h, _):
                    for src in range(1, nx):
                        blocks(work, src, h)
                    return 0

                lax.fori_loop(0, min(nz, AHEAD + 3), near, 0)

        if AHEAD + 3 < nz:
            @when((k > nk) & (s - nk + 2 < nz))
            def _():
                for src in range(1, nx):
                    blocks(project, src, s - nk + 2)
                    blocks(sum_cores, src, s - nk + 2)

        @when(s == nk + 0 + distance)
        def _():
            finish(0)

        @when(k == nk + 1 + jnp.maximum(distance - AHEAD - 2, 0))
        def _():
            for src in range(1, nx):
                finish(src)

        far_k = k - nz - 1

        @when(valid(far_k))
        def _():
            adjoint_filter(far_k)

        return 0

    lax.fori_loop(AHEAD, AHEAD + nk + nz + 1, step, 0)

    @when(stays)
    def _():
        yout[...] = yfs[...]

    @when(leaves)
    def _():
        def land(q, _):
            y_copy(q).wait()
            return 0

        lax.fori_loop(0, nk, land, 0)
        yout[...] = yfr[...]

    @when(leaves & on_line)
    def _():
        for h in range(halves):
            cot_copy(h).wait_send()

    @when(jnp.logical_not(on_line))
    def _():
        for h in range(halves):
            side_copy(h).wait_send()

    @when(side_leaves)
    def _():
        for h in range(halves):
            side_relay(h).wait_send()

    for h in range(halves):
        for d in range(ny):
            spread(d, h).wait_send()
        for d in range(1, ny):
            relay(d, h).wait_send()

    def drain(k, _):
        for d in range(1, nx):
            w_copy(d, k).wait_send()
        for slot in range(ny):
            a_copy((1 - c) * ny + slot, k).wait_send()
        for d in range(1, ny):
            b_copy(lax.rem(y + d, ny), k).wait_send()
        for o in range(nz):
            @when((z < nz - 1) & (o <= z))
            def _():
                x_copy(True, o, k).wait_send()

            @when((z > 0) & (o >= z))
            def _():
                x_copy(False, o, k).wait_send()

            @when(o > z)
            def _():
                d_copy(True, o, k).wait_send()

            @when(o < z)
            def _():
                d_copy(False, o, k).wait_send()

        for hop in range(1, hops + 1):
            @when(index + hop < ctx)
            def _():
                f_copy(hop, k).wait_send()

            @when(index - hop >= 0)
            def _():
                s_copy(hop, k).wait_send()

        return 0

    lax.fori_loop(0, nk, drain, 0)


def fused_call(sizes, lengths, tokens, cot, weight, parameters):
    nz, nx, ny, hops, modes = sizes
    length, channels = cot.shape
    width = weight.shape[1]
    nk = channels // COLS
    vmem = pl.BlockSpec(memory_space=pltpu.VMEM)
    hbm = pl.BlockSpec(memory_space=pl.ANY)
    token = jax.ShapeDtypeStruct((length, channels), BF16)
    dma = pltpu.SemaphoreType.DMA
    near = max(ny - 1, 1)
    wide_x = max(nx - 1, 1)
    flops = 8 * nz * length * channels * width * nx // 2
    return pl.pallas_call(
        functools.partial(fused, sizes),
        out_shape=(token,) * 4,
        in_specs=[pl.BlockSpec(memory_space=pltpu.SMEM)] + [vmem] * 3 + [hbm] * 2 + [vmem] * len(parameters),
        out_specs=(vmem,) * 4,
        scratch_shapes=[
            pltpu.VMEM((channels, width), BF16),
            pltpu.VMEM((wide_x, channels, width), BF16),
            pltpu.VMEM((nz, length, channels), BF16),
            pltpu.VMEM((nz, nz, length, COLS), F32),
            pltpu.VMEM((nz, nk, length, COLS), BF16),
            pltpu.VMEM((nz + 1, nk, length, COLS), BF16),
            pltpu.VMEM((nz, length, channels), BF16),
            pltpu.VMEM((ny, length, channels), BF16),
            pltpu.VMEM((ny, length, channels), BF16),
            pltpu.VMEM((near, length, channels), BF16),
            pltpu.VMEM((near, length, channels), BF16),
            pltpu.VMEM((ny, length, channels), F32),
            pltpu.VMEM((length, channels), F32),
            pltpu.VMEM((length, channels), BF16),
            pltpu.VMEM((length, channels), BF16),
            pltpu.VMEM((length, COLS), F32),
            pltpu.VMEM((length, channels), F32),
            pltpu.VMEM((length, channels), BF16),
            pltpu.VMEM((nk, modes, COLS), F32),
            pltpu.VMEM((hops, nk, modes, COLS), F32),
            pltpu.VMEM((nk, modes, COLS), F32),
            pltpu.VMEM((hops, nk, modes, COLS), F32),
            pltpu.VMEM((length, channels), BF16),
            pltpu.VMEM((channels // GSIZE * modes, LANES), F32),
            pltpu.VMEM((channels // GSIZE * modes, LANES), F32),
            pltpu.VMEM((1, length), F32),
            pltpu.VMEM((1, length), F32),
            pltpu.VMEM((length, length), F32),
            pltpu.VMEM((length, length), F32),
            dma((2,)),
            dma((PIECES,)), dma((PIECES,)),
            dma((wide_x, nk)), dma((wide_x, nk)),
            dma((PIECES,)), dma((PIECES,)),
            dma((ny, PIECES)), dma((ny, PIECES)),
            dma((near, PIECES)), dma((near, PIECES)),
            dma((2, nz, nk)), dma((nz, nk)),
            dma((nz, nk)), dma((nz + 1, nk)),
            dma((ny, nk)), dma((ny, nk)),
            dma((near, nk)), dma((near, nk)),
            dma((nk,)), dma((nk,)),
            dma((hops, nk)), dma((hops, nk)),
            dma((hops, nk)), dma((hops, nk)),
        ],
        compiler_params=pltpu.CompilerParams(
            collective_id=0, has_side_effects=True, vmem_limit_bytes=63 * 2**20
        ),
        cost_estimate=pl.CostEstimate(flops=flops, bytes_accessed=16 * 2**20, transcendentals=0),
    )(lengths, *tokens, cot, weight, *parameters)


def hand_over(results):
    count = len(results)
    length, channels = results[0].shape
    steps = 4

    def kernel(*refs):
        for i in range(count):
            refs[count + i][...] = refs[i][...]

    block = pl.BlockSpec((length // steps, channels), lambda i: (i, 0))
    size = sum(r.size * 2 for r in results)
    return pl.pallas_call(
        kernel,
        grid=(steps,),
        out_shape=tuple(jax.ShapeDtypeStruct(r.shape, r.dtype) for r in results),
        in_specs=[block] * count,
        out_specs=(block,) * count,
        cost_estimate=pl.CostEstimate(flops=0, bytes_accessed=2 * size, transcendentals=0),
    )(*results)


def on_device(
    query_branch,
    key_branch,
    value_branch,
    out_cotangent,
    out_weight,
    residues,
    decay_rates,
    skip_gains,
    record_lengths,
):
    length, channels = query_branch.shape
    modes = residues.shape[1]
    nz, nx, ny = lax.axis_size("z"), lax.axis_size("x"), lax.axis_size("y")
    ctx = nz * nx
    hops = -(-(length * ctx // 4) // length)

    rates = decay_rates.T
    coeffs = residues.T * jnp.sqrt(1.0 - jnp.exp(-2.0 * rates))
    results = fused_call(
        (nz, nx, ny, hops, modes),
        record_lengths,
        (query_branch, key_branch, value_branch), out_cotangent, out_weight,
        (rates, coeffs, skip_gains[None, :]),
    )
    return hand_over(results)


def solution(mesh):
    ctx, tp = mesh.devices.shape
    fine = Mesh(mesh.devices.reshape(tp, ctx // tp, tp // CORES, CORES), ("z", "x", "y", "c"))
    tokens = P(("z", "x"), ("y", "c"))
    placed = (
        tokens,
        tokens,
        tokens,
        tokens,
        P(("y", "c"), ("z", "x")),
        P(("y", "c"), None),
        P(("y", "c"), None),
        P(("y", "c")),
        P(),
    )
    return jax.shard_map(
        on_device,
        mesh=fine,
        in_specs=placed,
        out_specs=(tokens, tokens, tokens, tokens),
        check_vma=False,
    )
```
